128 devices in a mesh: clu: 32 (over z, x, core), frq: 4 (over y).
Axes of the slice: x: 4, y: 4, z: 4, core: 2. Of those that a mesh axis runs over, the one named last changes fastest.
Arguments:
- incident: float32 [4, 2, 65536, 128], P('frq', None, 'clu'), may hold values from -6 to 6
- initial: float32 [4, 2, 65536, 128], P('frq', None, 'clu'), may hold values from -3 to 3
- near_blocks: bfloat16 [512, 8, 4, 2, 128, 128], P('clu', None, 'frq'), may hold values from -0.125 to 0.125
- near_pattern: int32 [512, 8], P('clu'), may hold values from 0 to 47
- crack_blocks: bfloat16 [1024, 4, 2, 128, 128], P('clu', 'frq'), may hold values from -0.25 to 0.25
- crack_cluster: int32 [1024, 1], P('clu'), may hold values from 0 to 31; in each aligned block of 32 rows (0 to 31, 32 to 63, ...) at most 2 rows name the same one
- crack_source: int32 [1024], P('clu'), may hold values from 0 to 3
- crack_target: int32 [1024], P('clu'), may hold values from 0 to 15
- pulse_spectrum: float32 [4, 2], P('frq'), may hold values from -4 to 4
Outputs:
- scattered: float32 [4, 2, 65536, 128], P('frq', None, 'clu')
- time_trace: float32 [4, 65536, 128], P('frq', 'clu')
The draws below stay inside these ranges and needn't reach their ends.
Inputs may be any that keep to these rules, and one draw needn't show every extreme that they name: `crack_cluster`: in the rows of one cluster no source cluster is named more than 2 times, a bound that some block reaches.
All inputs are finite; a program needn't handle non-finite values.
Results may differ from the reference program's by a relative error of at most 0.0014.
Values may be sent and summed in bfloat16 or wider, within the bound.
A program may use at most 128 MiB of HBM per device.

```python
import math
import jax
import jax.numpy as jnp
import numpy as np
from jax import lax

BLK = 128
NB_DEV = 16
NEAR = 8
DIRS = 128
E_DEV = 32
FRONT = 4
CAP = 2
FREQ = 4
NBLK = 512
NPANEL = 65536
EDGES = 1024
NT = 4
N_CLU = 32


def set_ends(values, key, smallest, top_value):
    longest = values.shape.index(max(values.shape))
    spots = []
    for shift in (0, 1):
        where = [jax.random.randint(jax.random.fold_in(key, axis), (), 0, length) for axis, length in enumerate(values.shape)]
        where[longest] = (where[longest] + shift) % values.shape[longest]
        spots.append(tuple(where))
    return values.at[spots[0]].set(smallest).at[spots[1]].set(top_value)


def level_of(stream_key, shape, shards, low, high):
    factor_of, own = 1.0, jax.random.fold_in(stream_key, 6)
    for position, parts in shards:
        draws = jnp.exp(jax.random.uniform(jax.random.fold_in(own, position), (parts,), jnp.float32, low / len(shards), high / len(shards)))
        factor_of = factor_of * jnp.repeat(draws, shape[position] // parts).reshape([-1 if axis == position else 1 for axis in range(len(shape))])
    return factor_of


def routed_block(key, own, number, rows, amount, top, most, slope):
    order = jax.random.permutation(key, amount)
    heavy_load, usual = load_shares(amount, rows * top, most, slope, True), load_shares(amount, rows * top, most, slope, False)
    places = jnp.arange(amount)

    def named(tallies, rotation):
        used = int((tallies > 0).sum())
        fixed = max(1, used // 4)
        passed = fixed + (places - fixed + rotation * (used - fixed)) % max(1, amount - fixed)
        return jnp.zeros((amount,), jnp.int32).at[order[jnp.where(places < fixed, places, passed)]].set(jnp.asarray(tallies, jnp.int32))

    tallies = jnp.where(number % 4 == 0, named(heavy_load, number // 4), named(usual, number - number // 4 - 1))
    mixed = jax.random.permutation(jax.random.fold_in(own, 3), amount)
    giver, receiver = mixed[0:amount // 2 * 2:2], mixed[1:amount // 2 * 2:2]
    room = jnp.minimum(tallies[giver] - 1, most - tallies[receiver]) // 2
    room = jnp.where((giver == order[0]) | (receiver == order[0]) | (tallies[receiver] == 0), 0, jnp.maximum(room, 0))
    passed = jax.random.randint(jax.random.fold_in(own, 4), (amount // 2,), 0, 1 << 20) % (room + 1)
    tallies = tallies.at[giver].add(-passed).at[receiver].add(passed)
    members = jnp.searchsorted(jnp.cumsum(tallies), jnp.arange(rows * top), side="right").astype(jnp.int32)
    table = members.reshape(top, rows).T
    table = table[jax.random.permutation(jax.random.fold_in(own, 1), rows)]
    rotation = jax.random.randint(jax.random.fold_in(own, 2), (rows, 1), 0, top)
    return jnp.take_along_axis(table, (jnp.arange(top)[None, :] + rotation) % top, axis=1)


def load_shares(count, total, most, skew, full):
    loads = [(1 << 20) // math.isqrt(rank ** skew) + 1 for rank in range(1, count + 1)]
    largest = most if full else min(most, max(-(-total // count), total * loads[0] // sum(loads)))
    least = 1 if total - largest >= count - 1 else 0
    given, surplus = [largest] + [least] * (count - 1), total - largest - least * (count - 1)
    while surplus > 0:
        movable = [i for i in range(1, count) if given[i] < largest] or [i for i in range(1, count) if given[i] < most]
        mass, budget = sum([loads[i] for i in movable]), surplus
        for i in movable:
            extra = min(most - given[i], max(1, budget * loads[i] // mass), surplus)
            given[i] = given[i] + extra
            surplus = surplus - extra
    return np.array(given)


def centred(key, dims, scale, bound, pieces=(), kind=jnp.bfloat16):
    array = jax.random.normal(key, dims, jnp.float32) * scale
    if len(pieces) > 0:
        array = level_of(key, dims, pieces, -0.22, 0.18) * array
    return jnp.clip(array, min=-bound, max=bound).astype(kind)


def setup_inputs(seed: int = 0) -> dict:
    key_list = jax.random.split(jax.random.key(seed), 10)
    incident = centred(key_list[0], (FREQ, 2, NPANEL, DIRS), 1.0, 6.0, ((0, 4), (2, 32)), jnp.float32)
    initial = centred(key_list[1], (FREQ, 2, NPANEL, DIRS), 0.5, 3.0, ((0, 4), (2, 32)), jnp.float32)
    near_blocks = centred(key_list[2], (NBLK, NEAR, FREQ, 2, BLK, BLK), (2 * NEAR * BLK) ** -0.5, 0.125, ((0, 32), (2, 4)))
    near_pattern = set_ends(jax.random.randint(key_list[3], (NBLK, NEAR), 0, 3 * NB_DEV), jax.random.fold_in(key_list[3], 1), 0, (3 * NB_DEV) - 1).astype(jnp.int32)
    crack_blocks = centred(key_list[4], (EDGES, FREQ, 2, BLK, BLK), (4 * BLK) ** -0.5, 0.25, ((0, 32), (1, 4)))
    crack_cluster_keys = jax.random.split(jax.random.fold_in(key_list[5], 1), EDGES // E_DEV)
    crack_cluster_turns = jax.random.permutation(jax.random.fold_in(key_list[5], 3), EDGES // E_DEV)
    crack_cluster = jax.vmap(lambda own, number: routed_block(jax.random.fold_in(key_list[5], 2), own, number, E_DEV, N_CLU, 1, CAP, 2))(crack_cluster_keys, crack_cluster_turns).reshape((EDGES, 1))
    crack_source = set_ends(jax.random.randint(key_list[6], (EDGES,), 0, FRONT), jax.random.fold_in(key_list[6], 1), 0, FRONT - 1).astype(jnp.int32)
    crack_target = set_ends(jax.random.randint(key_list[7], (EDGES,), 0, NB_DEV), jax.random.fold_in(key_list[7], 1), 0, NB_DEV - 1).astype(jnp.int32)
    pulse_spectrum = centred(key_list[8], (FREQ, 2), 1.0, 4.0, ((0, 4),), jnp.float32)
    return dict(incident=incident, initial=initial, near_blocks=near_blocks, near_pattern=near_pattern, crack_blocks=crack_blocks, crack_cluster=crack_cluster, crack_source=crack_source, crack_target=crack_target, pulse_spectrum=pulse_spectrum)


epsilon = 1e-06

def complex_times(factor, vector):
    real_part = factor[0][:, None, :] * vector[:, 0] - factor[1][:, None, :] * vector[:, 1]
    imag_part = factor[0][:, None, :] * vector[:, 1] + factor[1][:, None, :] * vector[:, 0]
    return jnp.stack([real_part, imag_part], axis=1)

def inner_local(former, latter):
    real_part = lax.optimization_barrier(jnp.sum(former[:, 0] * latter[:, 0] + former[:, 1] * latter[:, 1], axis=1))
    imag_part = lax.optimization_barrier(jnp.sum(former[:, 0] * latter[:, 1] - former[:, 1] * latter[:, 0], axis=1))
    return (real_part, imag_part)

def square_local(vector):
    return lax.optimization_barrier(jnp.sum(vector[:, 0] * vector[:, 0] + vector[:, 1] * vector[:, 1], axis=1))

def least_squares(beta_norm, first_h, sub_one, second_h, third_h, sub_two):
    r_one = jnp.sqrt(first_h[0] ** 2 + first_h[1] ** 2 + sub_one ** 2)
    q_real = first_h[0] / r_one
    q_imag = first_h[1] / r_one
    q_low = sub_one / r_one
    mix_real = q_real * second_h[0] + q_imag * second_h[1] + q_low * third_h[0]
    mix_imag = q_real * second_h[1] - q_imag * second_h[0] + q_low * third_h[1]
    top_real = second_h[0] - (mix_real * q_real - mix_imag * q_imag)
    top_imag = second_h[1] - (mix_real * q_imag + mix_imag * q_real)
    mid_real = third_h[0] - mix_real * q_low
    mid_imag = third_h[1] - mix_imag * q_low
    r_two_sq = top_real ** 2 + top_imag ** 2 + mid_real ** 2 + mid_imag ** 2 + sub_two ** 2
    later_real = beta_norm * top_real / r_two_sq
    later_imag = -beta_norm * top_imag / r_two_sq
    early_real = (beta_norm * q_real - (mix_real * later_real - mix_imag * later_imag)) / r_one
    early_imag = (-beta_norm * q_imag - (mix_real * later_imag + mix_imag * later_real)) / r_one
    return ((early_real, early_imag), (later_real, later_imag))

def reference(incident, initial, near_blocks, near_pattern, crack_blocks, crack_cluster, crack_source, crack_target, pulse_spectrum):
    rows = jnp.arange(NBLK, dtype=jnp.int32)
    cluster_of = rows // NB_DEV
    columns = ((cluster_of[:, None] + near_pattern // NB_DEV - 1) % N_CLU * NB_DEV + near_pattern % NB_DEV).astype(jnp.int32)
    edge_rows = jnp.arange(EDGES, dtype=jnp.int32)
    targets = (edge_rows // E_DEV * NB_DEV + crack_target).astype(jnp.int32)
    sources = (crack_cluster[:, 0] * NB_DEV + crack_source).astype(jnp.int32)

    def apply(vector):
        low = vector.astype(jnp.bfloat16).reshape(FREQ, 2, NBLK, BLK, DIRS)

        def one_freq(freq_index):
            blocks = lax.dynamic_index_in_dim(near_blocks, freq_index, 2, keepdims=False).astype(jnp.float32)
            field = lax.dynamic_index_in_dim(low, freq_index, 0, keepdims=False).astype(jnp.float32)
            picked = field[:, columns]
            products = jnp.einsum('bscpq,dbsqk->cdbpk', blocks, picked)
            near_real = products[0, 0] - products[1, 1]
            near_imag = products[0, 1] + products[1, 0]
            couple = lax.dynamic_index_in_dim(crack_blocks, freq_index, 1, keepdims=False).astype(jnp.float32)
            chosen = field[:, sources]
            crack_prod = jnp.einsum('ecpq,deqk->cdepk', couple, chosen)
            crack_real = crack_prod[0, 0] - crack_prod[1, 1]
            crack_imag = crack_prod[0, 1] + crack_prod[1, 0]
            zeros = jnp.zeros((NBLK, BLK, DIRS), jnp.float32)
            total_real = near_real + zeros.at[targets].add(crack_real)
            total_imag = near_imag + zeros.at[targets].add(crack_imag)
            return jnp.stack([total_real, total_imag], axis=0)
        result = lax.map(one_freq, jnp.arange(FREQ, dtype=jnp.int32))
        return 0.5 * vector + result.reshape(FREQ, 2, NPANEL, DIRS)
    residual = incident - apply(initial)
    beta_norm = jnp.sqrt(square_local(residual) + epsilon)
    basis_one = residual / beta_norm[:, None, None, :]
    image = apply(basis_one)
    first_h = inner_local(basis_one, image)
    image = image - complex_times(first_h, basis_one)
    sub_one = jnp.sqrt(square_local(image) + epsilon)
    basis_two = image / sub_one[:, None, None, :]
    image = apply(basis_two)
    second_h = inner_local(basis_one, image)
    third_h = inner_local(basis_two, image)
    image = image - complex_times(second_h, basis_one) - complex_times(third_h, basis_two)
    sub_two = jnp.sqrt(square_local(image) + epsilon)
    early, later = least_squares(beta_norm, first_h, sub_one, second_h, third_h, sub_two)
    scattered = initial + complex_times(early, basis_one) + complex_times(later, basis_two)
    times = jnp.arange(NT, dtype=jnp.float32)[:, None]
    freqs = jnp.arange(FREQ, dtype=jnp.float32)[None, :]
    angle = 2.0 * jnp.pi * times * freqs / NT
    coef_real = pulse_spectrum[None, :, 0] * jnp.cos(angle) - pulse_spectrum[None, :, 1] * jnp.sin(angle)
    coef_imag = -(pulse_spectrum[None, :, 0] * jnp.sin(angle) + pulse_spectrum[None, :, 1] * jnp.cos(angle))
    time_trace = jnp.einsum('tf,fpk->tpk', coef_real, scattered[:, 0], precision=lax.Precision.HIGHEST)
    time_trace = time_trace + jnp.einsum('tf,fpk->tpk', coef_imag, scattered[:, 1], precision=lax.Precision.HIGHEST)
    return (scattered, time_trace)
```

```python
import functools

import jax
import jax.numpy as jnp
from jax import lax
from jax.experimental import pallas as pl
from jax.experimental.pallas import tpu as pltpu
from jax.sharding import PartitionSpec as P

MESH = pl.DeviceIdType.MESH
F32, BF16, I32 = jnp.float32, jnp.bfloat16, jnp.int32
EPS = 1e-06
BLK = 128
NB = 16
NEAR = 8
EDGES = 32
HALF = BLK // 2
SET = 8
PANELS = NB * BLK
NX = NZ = NY = 4
SPLIT = 6


def add4(a, d):
    return lax.rem(a + (d % 4), 4)


def kernel(
    pat, ccl, csrc, links, pulse, inc_hbm, ini_hbm, near_hbm, crack_hbm,
    scat_hbm, trace_hbm,
    A, C, R, X0, W, Y, prod, xe0, xe1, ag0, ag1,
    part2, sendp, sendm, half_in, full_in, far_r, far_w,
    rowbuf, colbuf, gbuf,
    load_sem, out_sem, ag_recv, ag_send, pair_recv, halo_recv, halo_send,
    y_recv, y_send, row_recv, row_send, col_recv, col_send, g_recv, g_send,
):
    me, yy = lax.axis_index("clu"), lax.axis_index("frq")
    core, xx = lax.rem(me, 2), lax.rem(lax.div(me, 2), 4)
    zz = lax.div(me, 8)
    spot = lax.rem(me, 8)

    def clu(dx, dz):
        return (add4(zz, dz) * 4 + add4(xx, dx)) * 2 + core

    partner = me + 1 - 2 * core
    right, left = lax.rem(me + 1, 32), lax.rem(me + 31, 32)

    def dev(c):
        return (c, yy)

    def ydev(dy):
        return (me, add4(yy, dy))

    def row_peer(i):
        return (me - spot + lax.rem(spot + i, 8), yy)

    def copy(src, dst, ssem, rsem, target):
        return pltpu.make_async_remote_copy(
            src_ref=src, dst_ref=dst, send_sem=ssem, recv_sem=rsem,
            device_id=target, device_id_type=MESH)

    def arrived(ref, ssem, rsem, source):
        copy(ref, ref, ssem, rsem, source).wait_recv()

    loads = [
        pltpu.make_async_copy(s, d, load_sem.at[i])
        for i, (s, d) in enumerate([(ini_hbm, X0), (near_hbm, A), (inc_hbm, R), (crack_hbm, C)])
    ]
    for l in loads:
        l.start()
    barrier = pltpu.get_barrier_semaphore()
    peers = [row_peer(i) for i in range(1, 8)]
    peers += [dev(clu(0, d)) for d in (1, 2, 3)]
    peers += [ydev(d) for d in (1, 2, 3)]
    peers += [dev(right), dev(left)]
    for p in peers:
        pl.semaphore_signal(barrier, inc=1, device_id=p, device_id_type=MESH)

    def rows_of(g):
        return pl.ds(pl.multiple_of(g * BLK, BLK), BLK)

    def put_low(re, im, g, xe, ag):
        low = jnp.concatenate([re.astype(BF16), im.astype(BF16)], axis=1)
        xe[NB + g] = low
        if ag is not None:
            ag[pl.ds(me * SET + 2 * g, 2)] = low.reshape(2, HALF, 2 * BLK)

    def gather_steps(parity, ag, group, off, n, x_first):
        hn = n // 2
        base = 22 * group

        def at(dp, ds):
            return clu(dp, ds) if x_first else clu(ds, dp)

        def region(c, part):
            start, length = {0: (off, n), 1: (off, hn), 2: (off + hn, hn)}[part]
            return ag.at[pl.ds(c * SET + start, length)]

        def send(c, part, target, slot):
            r = region(c, part)
            copy(r, r, ag_send.at[parity], ag_recv.at[parity, base + slot], dev(target)).start()

        def wait(c, part, source, slot):
            arrived(region(c, part), ag_send.at[parity], ag_recv.at[parity, base + slot], dev(source))

        def share(c, part):
            r = region(c, part)
            copy(r, r, ag_send.at[parity], pair_recv.at[parity], dev(partner)).start()

        cols = [0, -1, 1]

        def first():
            send(me, 0, at(1, 0), 0)
            send(me, 0, at(-1, 0), 1)
            send(me, 0, at(0, 1), 4)
            send(me, 0, at(0, -1), 5)
            share(me, 0)

        def primary(sign):
            def step():
                c = at(-sign, 0)
                wait(c, 0, c, 0 if sign > 0 else 1)
                send(c, 1 if sign > 0 else 2, at(sign, 0), 2 if sign > 0 else 3)
                k = 1 if sign > 0 else 2
                send(c, 0, at(0, 1), 4 + 4 * k)
                send(c, 0, at(0, -1), 5 + 4 * k)
                share(c, 0)
            return step

        def far(sign):
            def step():
                c, part = at(2, 0), 1 if sign > 0 else 2
                wait(c, part, at(-sign, 0), 2 if sign > 0 else 3)
                slot = 16 if sign > 0 else 18
                send(c, part, at(0, 1), slot)
                send(c, part, at(0, -1), slot + 1)
                share(c, part)
            return step

        def second(k, sign):
            def step():
                c = at(cols[k], -sign)
                wait(c, 0, at(0, -sign), 4 + 4 * k + (0 if sign > 0 else 1))
                send(c, 1 if sign > 0 else 2, at(0, sign), 6 + 4 * k + (0 if sign > 0 else 1))
                share(c, 0)
            return step

        def second_far(part, sign):
            def step():
                c = at(2, -sign)
                slot = 16 if part == 1 else 18
                wait(c, part, at(0, -sign), slot + (0 if sign > 0 else 1))
                if (part == 1) == (sign > 0):
                    send(c, part, at(0, sign), 20 if sign > 0 else 21)
                share(c, part)
            return step

        def final(k, sign):
            def step():
                c, part = at(2 if k == 3 else cols[k], 2), 1 if sign > 0 else 2
                slot = (20 if k == 3 else 6 + 4 * k) + (0 if sign > 0 else 1)
                wait(c, part, at(0, -sign), slot)
                share(c, part)
            return step

        early = [primary(1), primary(-1)]
        early += [second(0, 1), second(0, -1)]
        middle = [second(1, 1), second(1, -1), second(2, 1), second(2, -1), far(1), far(-1)]
        late = [second_far(1, 1), second_far(2, -1), second_far(1, -1), second_far(2, 1)]
        late += [final(k, s) for k in range(4) for s in (1, -1)]
        return first, early, middle, late

    def gather(parity, ag):
        groups = [(0, SPLIT, True), (SPLIT, SET - SPLIT, False)]
        made = [gather_steps(parity, ag, i, *g) for i, g in enumerate(groups) if g[1]]
        firsts = [m[0] for m in made]
        mixed = [[s for steps in zip(*[m[k] for m in made]) for s in steps] for k in (1, 2, 3)]
        total = 0
        for _, n, _ in groups:
            total += 15 * n + 16 * n

        def finish():
            arrived(ag.at[pl.ds(0, 16 * SET)], ag_send.at[parity], pair_recv.at[parity], dev(partner))

        def drain():
            r = ag.at[pl.ds(0, total)]
            copy(r, r, ag_send.at[parity], pair_recv.at[parity], dev(partner)).wait_send()

        return firsts, mixed, finish, drain

    def halo_start(parity, xe):
        own = xe.at[pl.ds(NB, NB)]
        copy(own, xe.at[pl.ds(0, NB)], halo_send.at[parity], halo_recv.at[parity, 0], dev(right)).start()
        copy(own, xe.at[pl.ds(2 * NB, NB)], halo_send.at[parity], halo_recv.at[parity, 1], dev(left)).start()

    def halo_wait(parity, xe):
        arrived(xe.at[pl.ds(0, NB)], halo_send.at[parity], halo_recv.at[parity, 0], dev(left))
        arrived(xe.at[pl.ds(2 * NB, NB)], halo_send.at[parity], halo_recv.at[parity, 1], dev(right))

    def halo_drain(parity, xe):
        r = xe.at[pl.ds(0, 2 * NB)]
        copy(r, r, halo_send.at[parity], halo_recv.at[parity, 0], dev(right)).wait_send()

    def near_products(xe, steps):
        places = {}
        for i, s in enumerate(steps):
            places.setdefault(i * NB // len(steps), []).append(s)

        def row(g, carry):
            for k, todo in places.items():
                @pl.when(g == k)
                def _(todo=todo):
                    for s in todo:
                        s()
            acc = None
            for p in range(NEAR // 2):
                xs = jnp.concatenate([xe[pat[g, 2 * p]], xe[pat[g, 2 * p + 1]]], axis=0)
                ms = jnp.concatenate([A[g * NEAR + 2 * p], A[g * NEAR + 2 * p + 1]], axis=1)
                d = jnp.dot(ms, xs, preferred_element_type=F32)
                acc = d if acc is None else acc + d
            r = rows_of(g)
            Y[0, r, :] = acc[:BLK, :BLK] - acc[BLK:, BLK:]
            Y[1, r, :] = acc[:BLK, BLK:] + acc[BLK:, :BLK]
            return carry

        lax.fori_loop(0, NB, row, 0)

    def crack_products(ag):
        def edge(e, carry):
            q = ccl[e, 0] * 4 + csrc[e]
            xc = jnp.concatenate([ag[2 * q], ag[2 * q + 1]], axis=0)
            turned = jnp.concatenate([-xc[:, BLK:], xc[:, :BLK]], axis=1)
            xs = jnp.concatenate([xc, turned], axis=0)
            ms = jnp.concatenate([C[e, :BLK, :], C[e, BLK:, :]], axis=1)
            prod[e] = jnp.dot(ms, xs, preferred_element_type=F32) + prod[links[e]]
            return carry

        lax.fori_loop(0, EDGES, edge, 0)

    def total_of(g):
        r = rows_of(g)
        d = prod[links[EDGES + g]]
        return Y[0, r, :] + d[:, :BLK], Y[1, r, :] + d[:, BLK:]

    def fold(v):
        return jnp.sum(v.reshape(BLK // 8, 8, BLK), axis=0)

    zero8 = jnp.zeros((8, BLK), F32)

    def line(v):
        return jnp.sum(v, axis=0, keepdims=True)

    def clu_sum(k, lines):
        pad = [jnp.zeros((1, BLK), F32)] * (8 - len(lines))
        rowbuf[k, spot] = jnp.concatenate(lines + pad, axis=0)
        for i in range(1, 8):
            copy(rowbuf.at[k, spot], rowbuf.at[k, spot], row_send.at[k], row_recv.at[k], row_peer(i)).start()
        seven = rowbuf.at[k, pl.ds(0, 7)]
        copy(seven, seven, row_send.at[k], row_recv.at[k], row_peer(1)).wait()
        s = rowbuf[k, 0]
        for i in range(1, 8):
            s = s + rowbuf[k, i]
        colbuf[k, zz] = s
        for d in (1, 2, 3):
            copy(colbuf.at[k, zz], colbuf.at[k, zz], col_send.at[k], col_recv.at[k], dev(clu(0, d))).start()
        three = colbuf.at[k, pl.ds(0, 3)]
        copy(three, three, col_send.at[k], col_recv.at[k], dev(clu(0, 1))).wait()
        s = (colbuf[k, 0] + colbuf[k, 1]) + (colbuf[k, 2] + colbuf[k, 3])
        return [s[i:i + 1, :] for i in range(len(lines))]

    def far_steps(k, xe, dest):
        own = xe.at[pl.ds(NB, NB)]

        def first():
            copy(own, dest.at[0], y_send.at[k], y_recv.at[k, 0], ydev(1)).start()
            copy(own, dest.at[1], y_send.at[k], y_recv.at[k, 1], ydev(-1)).start()

        def up():
            arrived(dest.at[0], y_send.at[k], y_recv.at[k, 0], ydev(-1))
            copy(dest.at[0, pl.ds(0, NB // 2)], dest.at[2, pl.ds(0, NB // 2)],
                 y_send.at[k], y_recv.at[k, 2], ydev(1)).start()

        def down():
            arrived(dest.at[1], y_send.at[k], y_recv.at[k, 1], ydev(1))
            copy(dest.at[1, pl.ds(NB // 2, NB // 2)], dest.at[2, pl.ds(NB // 2, NB // 2)],
                 y_send.at[k], y_recv.at[k, 3], ydev(-1)).start()

        def done():
            arrived(dest.at[2, pl.ds(0, NB // 2)], y_send.at[k], y_recv.at[k, 2], ydev(-1))
            arrived(dest.at[2, pl.ds(NB // 2, NB // 2)], y_send.at[k], y_recv.at[k, 3], ydev(1))
            for i in (0, 1):
                pass
            r = dest.at[pl.ds(0, 3)]
            copy(r, r, y_send.at[k], y_recv.at[k, 0], ydev(1)).wait_send()

        return first, up, down, done

    def coef(t, f, pr, pi):
        m = lax.rem(t * f, 4)
        cs = jnp.where(m == 0, 1.0, jnp.where(m == 2, -1.0, 0.0)).astype(F32)
        sn = jnp.where(m == 1, 1.0, jnp.where(m == 3, -1.0, 0.0)).astype(F32)
        return pr * cs - pi * sn, -(pr * sn + pi * cs)

    own_pr, own_pi = pulse[0, 0], pulse[0, 1]
    MID = PANELS // 2

    def share_first():
        cr, ci = coef(add4(yy, 2), yy, own_pr, own_pi)

        def body(g, carry):
            r = rows_of(g)
            part2[r, :] = cr * X0[0, r, :] + ci * X0[1, r, :]
            return carry

        lax.fori_loop(0, NB, body, 0)
        lo, hi = part2.at[pl.ds(0, MID)], part2.at[pl.ds(MID, MID)]
        copy(lo, half_in.at[0], y_send.at[0], y_recv.at[0, 0], ydev(1)).start()
        copy(hi, half_in.at[1], y_send.at[0], y_recv.at[0, 1], ydev(-1)).start()

    def share_second():
        crp, cip = coef(add4(yy, 1), yy, own_pr, own_pi)
        crm, cim = coef(add4(yy, 3), yy, own_pr, own_pi)
        arrived(half_in.at[0], y_send.at[0], y_recv.at[0, 0], ydev(-1))
        arrived(half_in.at[1], y_send.at[0], y_recv.at[0, 1], ydev(1))

        def body(g, carry):
            r, q = rows_of(g), rows_of(g + NB // 2)
            a, b = X0[0, r, :], X0[1, r, :]
            sendp[r, :] = crp * a + cip * b + half_in[0, r, :]
            sendm[r, :] = crm * a + cim * b
            a, b = X0[0, q, :], X0[1, q, :]
            sendp[q, :] = crp * a + cip * b
            sendm[q, :] = crm * a + cim * b + half_in[1, r, :]
            return carry

        lax.fori_loop(0, NB // 2, body, 0)
        copy(sendp, full_in.at[0], y_send.at[3], y_recv.at[0, 2], ydev(1)).start()
        copy(sendm, full_in.at[1], y_send.at[3], y_recv.at[0, 3], ydev(-1)).start()

    def share_done():
        arrived(full_in.at[0], y_send.at[3], y_recv.at[0, 2], ydev(-1))
        arrived(full_in.at[1], y_send.at[3], y_recv.at[0, 3], ydev(1))
        copy(part2, part2, y_send.at[0], y_recv.at[0, 0], ydev(1)).wait_send()
        copy(full_in, full_in, y_send.at[3], y_recv.at[0, 0], ydev(1)).wait_send()

    def apply(parity, xe, ag, plan, y_steps):
        firsts, mixed, finish, drain = plan
        early, middle, late = mixed
        for s in early:
            s()
        for s in y_steps[:1]:
            s()
        for s in middle:
            s()
        halo_wait(parity, xe)
        near_products(xe, late + list(y_steps[1:]))
        finish()
        crack_products(ag)
        drain()
        halo_drain(parity, xe)

    loads[0].wait()

    def low_front(g, carry):
        r = rows_of(g)
        put_low(X0[0, r, :], X0[1, r, :], g, xe0, ag0)
        return carry

    def low_rest(g, carry):
        r = rows_of(g)
        put_low(X0[0, r, :], X0[1, r, :], g, xe0, None)
        return carry

    lax.fori_loop(0, 4, low_front, 0)
    pl.semaphore_wait(barrier, len(peers))
    plan = gather(0, ag0)
    for s in plan[0]:
        s()
    lax.fori_loop(4, NB, low_rest, 0)
    halo_start(0, xe0)
    share_first()

    prod[EDGES] = jnp.zeros((BLK, 2 * BLK), F32)
    loads[1].wait()
    loads[2].wait()
    loads[3].wait()

    apply(0, xe0, ag0, plan, (share_second, share_done))

    def residual(g, acc, ag):
        r = rows_of(g)
        nr, ni = total_of(g)
        re = R[0, r, :] - (0.5 * X0[0, r, :] + nr)
        im = R[1, r, :] - (0.5 * X0[1, r, :] + ni)
        R[0, r, :] = re
        R[1, r, :] = im
        put_low(re, im, g, xe1, ag)
        return acc + fold(re * re + im * im)

    acc = lax.fori_loop(0, 4, lambda g, a: residual(g, a, ag1), zero8)
    plan = gather(1, ag1)
    for s in plan[0]:
        s()
    rr = lax.fori_loop(4, NB, lambda g, a: residual(g, a, None), acc)
    halo_start(1, xe1)
    y_first, y_up, y_down, y_done = far_steps(1, xe1, far_r)
    y_first()
    rr = line(rr)

    apply(1, xe1, ag1, plan, (lambda: None, y_up, y_down, y_done))

    def image(g, acc):
        r = rows_of(g)
        nr, ni = total_of(g)
        vr, vi = R[0, r, :], R[1, r, :]
        wr, wi = 0.5 * vr + nr, 0.5 * vi + ni
        W[0, r, :] = wr
        W[1, r, :] = wi
        return acc[0] + fold(vr * wr + vi * wi), acc[1] + fold(vr * wi - vi * wr)

    pr, pi = lax.fori_loop(0, NB, image, (zero8, zero8))
    rr, pr, pi = clu_sum(0, [rr, line(pr), line(pi)])
    beta2 = rr + EPS
    h11r, h11i = pr / beta2, pi / beta2

    def ortho(g, acc, ag):
        r = rows_of(g)
        vr, vi = R[0, r, :], R[1, r, :]
        wr = W[0, r, :] - (h11r * vr - h11i * vi)
        wi = W[1, r, :] - (h11r * vi + h11i * vr)
        W[0, r, :] = wr
        W[1, r, :] = wi
        put_low(wr, wi, g, xe0, ag)
        return (acc[0] + fold(wr * wr + wi * wi), acc[1] + fold(vr * wr + vi * wi),
                acc[2] + fold(vr * wi - vi * wr))

    acc = lax.fori_loop(0, 4, lambda g, a: ortho(g, a, ag0), (zero8,) * 3)
    plan = gather(0, ag0)
    for s in plan[0]:
        s()
    ww, gr, gi = lax.fori_loop(4, NB, lambda g, a: ortho(g, a, None), acc)
    halo_start(0, xe0)
    y_first, y_up, y_down, y_done = far_steps(2, xe0, far_w)
    y_first()

    apply(0, xe0, ag0, plan, (lambda: None, y_up, y_down, y_done))

    def heights(g, acc):
        r = rows_of(g)
        nr, ni = total_of(g)
        vr, vi, wr, wi = R[0, r, :], R[1, r, :], W[0, r, :], W[1, r, :]
        ur, ui = 0.5 * wr + nr, 0.5 * wi + ni
        new = (vr * ur + vi * ui, vr * ui - vi * ur, wr * ur + wi * ui, wr * ui - wi * ur, ur * ur + ui * ui)
        return tuple(a + fold(n) for a, n in zip(acc, new))

    sums = lax.fori_loop(0, NB, heights, (zero8,) * 5)
    ww, gr, gi, ar, ai, br, bi, uu = clu_sum(1, [line(v) for v in (ww, gr, gi) + sums])

    beta = jnp.sqrt(beta2)
    inv_b = 1.0 / beta
    h21 = jnp.sqrt(ww / beta2 + EPS)
    scale2 = inv_b / h21
    n1, n2 = rr * (inv_b * inv_b), ww * (scale2 * scale2)
    cross = inv_b * scale2
    h12r, h12i, g12r, g12i = ar * cross, ai * cross, gr * cross, gi * cross
    sq2 = scale2 * scale2
    h22r, h22i, un = br * sq2, bi * sq2, uu * sq2
    m12, m22 = h12r * h12r + h12i * h12i, h22r * h22r + h22i * h22i
    mixr, mixi = h12r * h22r + h12i * h22i, h12r * h22i - h12i * h22r
    rest = un + m12 * (n1 - 2.0) + m22 * (n2 - 2.0) + 2.0 * (mixr * g12r - mixi * g12i)
    h32 = jnp.sqrt(jnp.maximum(rest, 0.0) + EPS)

    r_one = jnp.sqrt(h11r * h11r + h11i * h11i + h21 * h21)
    q_real, q_imag, q_low = h11r / r_one, h11i / r_one, h21 / r_one
    mix_real = q_real * h12r + q_imag * h12i + q_low * h22r
    mix_imag = q_real * h12i - q_imag * h12r + q_low * h22i
    top_real = h12r - (mix_real * q_real - mix_imag * q_imag)
    top_imag = h12i - (mix_real * q_imag + mix_imag * q_real)
    mid_real, mid_imag = h22r - mix_real * q_low, h22i - mix_imag * q_low
    r_two_sq = top_real**2 + top_imag**2 + mid_real**2 + mid_imag**2 + h32 * h32
    y2r, y2i = beta * top_real / r_two_sq, -beta * top_imag / r_two_sq
    y1r = (beta * q_real - (mix_real * y2r - mix_imag * y2i)) / r_one
    y1i = (-beta * q_imag - (mix_real * y2i + mix_imag * y2r)) / r_one
    a1r, a1i, a2r, a2i = y1r * inv_b, y1i * inv_b, y2r * scale2, y2i * scale2

    ones = jnp.ones((1, BLK), F32)
    blank = jnp.zeros((1, BLK), F32)
    gbuf[yy] = jnp.concatenate([a1r, a1i, a2r, a2i, own_pr * ones, own_pi * ones, blank, blank], axis=0)
    for d in (1, 2, 3):
        copy(gbuf.at[yy], gbuf.at[yy], g_send.at[0], g_recv.at[0], ydev(d)).start()

    def solve(g, carry):
        r = rows_of(g)
        vr, vi, wr, wi = R[0, r, :], R[1, r, :], W[0, r, :], W[1, r, :]
        X0[0, r, :] = X0[0, r, :] + (a1r * vr - a1i * vi) + (a2r * wr - a2i * wi)
        X0[1, r, :] = X0[1, r, :] + (a1r * vi + a1i * vr) + (a2r * wi + a2i * wr)
        return carry

    lax.fori_loop(0, NB, solve, 0)
    out_scat = pltpu.make_async_copy(X0, scat_hbm, out_sem.at[0])
    out_scat.start()
    three = gbuf.at[pl.ds(0, 3)]
    copy(three, three, g_send.at[0], g_recv.at[0], ydev(1)).wait()

    own_cr, own_ci = coef(yy, yy, own_pr, own_pi)
    factors = []
    for d in (-1, 1, 2):
        f = add4(yy, d)
        b = gbuf[f]
        cr, ci = coef(yy, f, b[4:5, :], b[5:6, :])
        for k in (0, 2):
            er, ei = b[k:k + 1, :], b[k + 1:k + 2, :]
            factors.append((cr * er + ci * ei, ci * er - cr * ei))

    def trace(g, carry):
        r = rows_of(g)
        t = full_in[0, r, :] + full_in[1, r, :] + (own_cr * X0[0, r, :] + own_ci * X0[1, r, :])
        for i in range(3):
            for k, store in enumerate((far_r, far_w)):
                v = store[i, g].astype(F32)
                fr, fi = factors[2 * i + k]
                t = t + (fr * v[:, :BLK] + fi * v[:, BLK:])
        part2[r, :] = t
        return carry

    lax.fori_loop(0, NB, trace, 0)
    out_trace = pltpu.make_async_copy(part2, trace_hbm, out_sem.at[1])
    out_trace.start()
    out_scat.wait()
    out_trace.wait()


def local(incident, initial, near_blocks, near_pattern, crack_blocks, crack_cluster, crack_source, crack_target, pulse):
    vmem, dma = pltpu.VMEM, pltpu.SemaphoreType.DMA
    hbm, smem = pl.BlockSpec(memory_space=pl.ANY), pl.BlockSpec(memory_space=pltpu.SMEM)
    vec = (2, PANELS, BLK)
    scratch = [
        vmem((NB * NEAR, 2 * BLK, BLK), BF16),
        vmem((EDGES, 2 * BLK, BLK), BF16),
        vmem(vec, F32), vmem(vec, F32), vmem(vec, F32), vmem(vec, F32),
        vmem((EDGES + 1, BLK, 2 * BLK), F32),
        vmem((3 * NB, BLK, 2 * BLK), BF16), vmem((3 * NB, BLK, 2 * BLK), BF16),
        vmem((32 * SET, HALF, 2 * BLK), BF16), vmem((32 * SET, HALF, 2 * BLK), BF16),
        vmem((PANELS, BLK), F32), vmem((PANELS, BLK), F32), vmem((PANELS, BLK), F32),
        vmem((2, PANELS // 2, BLK), F32), vmem((2, PANELS, BLK), F32),
        vmem((3, NB, BLK, 2 * BLK), BF16), vmem((3, NB, BLK, 2 * BLK), BF16),
        vmem((2, 8, 8, BLK), F32), vmem((2, 4, 8, BLK), F32), vmem((4, 8, BLK), F32),
        dma((4,)), dma((2,)), dma((2, 44)), dma((2,)), dma((2,)), dma((2, 2)), dma((2,)),
        dma((3, 4)), dma((4,)), dma((2,)), dma((2,)), dma((2,)), dma((2,)), dma((1,)), dma((1,)),
    ]
    place = jnp.arange(EDGES + NB, dtype=I32)
    target = jnp.where(place < EDGES, jnp.pad(crack_target, (0, NB)), place - EDGES)
    each = jnp.arange(EDGES, dtype=I32)
    found = (crack_target[None, :] == target[:, None]) & (each[None, :] < place[:, None])
    links = jnp.max(jnp.where(found, each[None, :], -1), axis=1)
    links = jnp.where(links < 0, EDGES, links)
    scattered, trace = pl.pallas_call(
        kernel,
        out_shape=(jax.ShapeDtypeStruct(vec, F32), jax.ShapeDtypeStruct((PANELS, BLK), F32)),
        in_specs=[smem] * 5 + [hbm] * 4,
        out_specs=(hbm, hbm),
        scratch_shapes=scratch,
        compiler_params=pltpu.CompilerParams(
            collective_id=0, has_side_effects=True, vmem_limit_bytes=66_000_000),
        name="gmres",
    )(
        near_pattern, crack_cluster, crack_source, links, pulse,
        incident.reshape(vec), initial.reshape(vec),
        near_blocks.reshape(NB * NEAR, 2 * BLK, BLK), crack_blocks.reshape(EDGES, 2 * BLK, BLK),
    )
    return scattered[None], trace[None]


def solution(mesh):
    in_specs = (
        P("frq", None, "clu", None),
        P("frq", None, "clu", None),
        P("clu", None, "frq", None, None, None),
        P("clu", None),
        P("clu", "frq", None, None, None),
        P("clu", None),
        P("clu"),
        P("clu"),
        P("frq", None),
    )
    out_specs = (P("frq", None, "clu", None), P("frq", "clu", None))
    return jax.shard_map(local, mesh=mesh, in_specs=in_specs, out_specs=out_specs, check_vma=False)
```

```python
import functools

import jax
import jax.numpy as jnp
from jax import lax
from jax.experimental import pallas as pl
from jax.experimental.pallas import tpu as pltpu
from jax.sharding import PartitionSpec as P

MESH = pl.DeviceIdType.MESH
F32, BF16, I32 = jnp.float32, jnp.bfloat16, jnp.int32
EPS = 1e-06
BLK = 128
NB = 16
NEAR = 8
EDGES = 32
HALF = BLK // 2
SET = 8
PANELS = NB * BLK
NX = NZ = NY = 4
PIECES = 4
SPLIT = 4


def add4(a, d):
    return lax.rem(a + (d % 4), 4)


def kernel(
    pat, ccl, csrc, links, pulse, inc_hbm, ini_hbm, near_hbm, crack_hbm,
    scat_hbm, trace_hbm,
    A, C, R, X0, W, Y, prod, xe0, xe1, ag0, ag1,
    part2, sendp, sendm, half_in, full_in, far_r, far_w,
    rowbuf, colbuf, gbuf,
    load_sem, out_sem, ag_recv, ag_send, pair_recv, halo_recv, halo_send,
    y_recv, y_send, row_recv, row_send, col_recv, col_send, g_recv, g_send,
):
    me, yy = lax.axis_index("clu"), lax.axis_index("frq")
    core, xx = lax.rem(me, 2), lax.rem(lax.div(me, 2), 4)
    zz = lax.div(me, 8)
    spot = lax.rem(me, 8)

    def clu(dx, dz):
        return (add4(zz, dz) * 4 + add4(xx, dx)) * 2 + core

    partner = me + 1 - 2 * core
    right, left = lax.rem(me + 1, 32), lax.rem(me + 31, 32)

    def dev(c):
        return (c, yy)

    def ydev(dy):
        return (me, add4(yy, dy))

    def row_peer(i):
        return (me - spot + lax.rem(spot + i, 8), yy)

    def copy(src, dst, ssem, rsem, target):
        return pltpu.make_async_remote_copy(
            src_ref=src, dst_ref=dst, send_sem=ssem, recv_sem=rsem,
            device_id=target, device_id_type=MESH)

    def arrived(ref, ssem, rsem, source):
        copy(ref, ref, ssem, rsem, source).wait_recv()

    loads = [
        pltpu.make_async_copy(s, d, load_sem.at[i])
        for i, (s, d) in enumerate([(ini_hbm, X0), (near_hbm, A), (inc_hbm, R), (crack_hbm, C)])
    ]
    for l in loads:
        l.start()
    barrier = pltpu.get_barrier_semaphore()
    peers = [row_peer(i) for i in range(1, 8)]
    peers += [dev(clu(0, d)) for d in (1, 2, 3)]
    peers += [ydev(d) for d in (1, 2, 3)]
    peers += [dev(right), dev(left)]
    for p in peers:
        pl.semaphore_signal(barrier, inc=1, device_id=p, device_id_type=MESH)

    def rows_of(g):
        return pl.ds(pl.multiple_of(g * BLK, BLK), BLK)

    def put_low(re, im, g, xe, ag):
        low = jnp.concatenate([re.astype(BF16), im.astype(BF16)], axis=1)
        xe[NB + g] = low
        if ag is not None:
            ag[pl.ds(me * SET + 2 * g, 2)] = low.reshape(2, HALF, 2 * BLK)

    def gather_steps(parity, ag, group, off, n, x_first):
        hn = n // 2
        base = 22 * group

        def at(dp, ds):
            return clu(dp, ds) if x_first else clu(ds, dp)

        def region(c, part):
            start, length = {0: (off, n), 1: (off, hn), 2: (off + hn, hn)}[part]
            return ag.at[pl.ds(c * SET + start, length)]

        def send(c, part, target, slot):
            r = region(c, part)
            copy(r, r, ag_send.at[parity], ag_recv.at[parity, base + slot], dev(target)).start()

        def wait(c, part, source, slot):
            arrived(region(c, part), ag_send.at[parity], ag_recv.at[parity, base + slot], dev(source))

        def share(c, part):
            r = region(c, part)
            copy(r, r, ag_send.at[parity], pair_recv.at[parity], dev(partner)).start()

        cols = [0, -1, 1]

        def first():
            send(me, 0, at(1, 0), 0)
            send(me, 0, at(-1, 0), 1)
            send(me, 0, at(0, 1), 4)
            send(me, 0, at(0, -1), 5)
            share(me, 0)

        def primary(sign):
            def step():
                c = at(-sign, 0)
                wait(c, 0, c, 0 if sign > 0 else 1)
                send(c, 1 if sign > 0 else 2, at(sign, 0), 2 if sign > 0 else 3)
                k = 1 if sign > 0 else 2
                send(c, 0, at(0, 1), 4 + 4 * k)
                send(c, 0, at(0, -1), 5 + 4 * k)
                share(c, 0)
            return step

        def far(sign):
            def step():
                c, part = at(2, 0), 1 if sign > 0 else 2
                wait(c, part, at(-sign, 0), 2 if sign > 0 else 3)
                slot = 16 if sign > 0 else 18
                send(c, part, at(0, 1), slot)
                send(c, part, at(0, -1), slot + 1)
                share(c, part)
            return step

        def second(k, sign):
            def step():
                c = at(cols[k], -sign)
                wait(c, 0, at(0, -sign), 4 + 4 * k + (0 if sign > 0 else 1))
                send(c, 1 if sign > 0 else 2, at(0, sign), 6 + 4 * k + (0 if sign > 0 else 1))
                share(c, 0)
            return step

        def second_far(part, sign):
            def step():
                c = at(2, -sign)
                slot = 16 if part == 1 else 18
                wait(c, part, at(0, -sign), slot + (0 if sign > 0 else 1))
                if (part == 1) == (sign > 0):
                    send(c, part, at(0, sign), 20 if sign > 0 else 21)
                share(c, part)
            return step

        def final(k, sign):
            def step():
                c, part = at(2 if k == 3 else cols[k], 2), 1 if sign > 0 else 2
                slot = (20 if k == 3 else 6 + 4 * k) + (0 if sign > 0 else 1)
                wait(c, part, at(0, -sign), slot)
                share(c, part)
            return step

        early = [primary(1), primary(-1)]
        early += [second(0, 1), second(0, -1)]
        middle = [second(1, 1), second(1, -1), second(2, 1), second(2, -1), far(1), far(-1)]
        middle += [second_far(1, 1), second_far(2, -1)]
        late = [second_far(1, -1), second_far(2, 1)]
        late += [final(k, s) for k in range(4) for s in (1, -1)]
        return first, early, middle, late

    def gather(parity, ag):
        groups = [(0, SPLIT, True), (SPLIT, SET - SPLIT, False)]
        made = [gather_steps(parity, ag, i, *g) for i, g in enumerate(groups) if g[1]]
        firsts = [m[0] for m in made]
        mixed = [[s for steps in zip(*[m[k] for m in made]) for s in steps] for k in (1, 2, 3)]
        total = 0
        for _, n, _ in groups:
            total += 15 * n + 16 * n

        def finish():
            arrived(ag.at[pl.ds(0, 16 * SET)], ag_send.at[parity], pair_recv.at[parity], dev(partner))

        def drain():
            r = ag.at[pl.ds(0, total)]
            copy(r, r, ag_send.at[parity], pair_recv.at[parity], dev(partner)).wait_send()

        return firsts, mixed, finish, drain

    def halo_start(parity, xe, piece):
        size = NB // PIECES
        own = xe.at[pl.ds(NB + piece * size, size)]
        for side, start, target in ((0, 0, right), (1, 2 * NB, left)):
            there = xe.at[pl.ds(start + piece * size, size)]
            copy(own, there, halo_send.at[parity], halo_recv.at[parity, side], dev(target)).start()

    def halo_wait(parity, xe):
        arrived(xe.at[pl.ds(0, NB)], halo_send.at[parity], halo_recv.at[parity, 0], dev(left))
        arrived(xe.at[pl.ds(2 * NB, NB)], halo_send.at[parity], halo_recv.at[parity, 1], dev(right))

    def halo_drain(parity, xe):
        r = xe.at[pl.ds(0, 2 * NB)]
        copy(r, r, halo_send.at[parity], halo_recv.at[parity, 0], dev(right)).wait_send()

    def near_products(xe, steps):
        places = {}
        for i, s in enumerate(steps):
            places.setdefault(i * NB // len(steps), []).append(s)

        def row(g, carry):
            for k, todo in places.items():
                @pl.when(g == k)
                def _(todo=todo):
                    for s in todo:
                        s()
            acc = None
            for p in range(NEAR // 2):
                xs = jnp.concatenate([xe[pat[2 * p, g]], xe[pat[2 * p + 1, g]]], axis=0)
                ms = jnp.concatenate([A[g * NEAR + 2 * p], A[g * NEAR + 2 * p + 1]], axis=1)
                d = jnp.dot(ms, xs, preferred_element_type=F32)
                acc = d if acc is None else acc + d
            r = rows_of(g)
            Y[0, r, :] = acc[:BLK, :BLK] - acc[BLK:, BLK:]
            Y[1, r, :] = acc[:BLK, BLK:] + acc[BLK:, :BLK]
            return carry

        lax.fori_loop(0, NB, row, 0)

    def crack_products(ag):
        def edge(e, carry):
            q = ccl[0, e] * 4 + csrc[e]
            xc = jnp.concatenate([ag[2 * q], ag[2 * q + 1]], axis=0)
            turned = jnp.concatenate([-xc[:, BLK:], xc[:, :BLK]], axis=1)
            xs = jnp.concatenate([xc, turned], axis=0)
            ms = jnp.concatenate([C[e, :BLK, :], C[e, BLK:, :]], axis=1)
            prod[e] = jnp.dot(ms, xs, preferred_element_type=F32) + prod[links[e]]
            return carry

        lax.fori_loop(0, EDGES, edge, 0)

    def total_of(g):
        r = rows_of(g)
        d = prod[links[EDGES + g]]
        return Y[0, r, :] + d[:, :BLK], Y[1, r, :] + d[:, BLK:]

    def fold(v):
        return jnp.sum(v.reshape(BLK // 8, 8, BLK), axis=0)

    zero8 = jnp.zeros((8, BLK), F32)

    def line(v):
        return jnp.sum(v, axis=0, keepdims=True)

    def clu_sum(k, lines):
        pad = [jnp.zeros((1, BLK), F32)] * (8 - len(lines))
        rowbuf[k, spot] = jnp.concatenate(lines + pad, axis=0)
        for i in range(1, 8):
            copy(rowbuf.at[k, spot], rowbuf.at[k, spot], row_send.at[k], row_recv.at[k], row_peer(i)).start()

        def cols():
            seven = rowbuf.at[k, pl.ds(0, 7)]
            copy(seven, seven, row_send.at[k], row_recv.at[k], row_peer(1)).wait()
            s = rowbuf[k, 0]
            for i in range(1, 8):
                s = s + rowbuf[k, i]
            colbuf[k, zz] = s
            for d in (1, 2, 3):
                copy(colbuf.at[k, zz], colbuf.at[k, zz], col_send.at[k], col_recv.at[k], dev(clu(0, d))).start()

        def end():
            three = colbuf.at[k, pl.ds(0, 3)]
            copy(three, three, col_send.at[k], col_recv.at[k], dev(clu(0, 1))).wait()
            s = (colbuf[k, 0] + colbuf[k, 1]) + (colbuf[k, 2] + colbuf[k, 3])
            return [s[i:i + 1, :] for i in range(len(lines))]

        return cols, end

    def far_steps(k, xe, dest):
        own = xe.at[pl.ds(NB, NB)]

        def first():
            copy(own, dest.at[0], y_send.at[k], y_recv.at[k, 0], ydev(1)).start()
            copy(own, dest.at[1], y_send.at[k], y_recv.at[k, 1], ydev(-1)).start()

        def up():
            arrived(dest.at[0], y_send.at[k], y_recv.at[k, 0], ydev(-1))
            copy(dest.at[0, pl.ds(0, NB // 2)], dest.at[2, pl.ds(0, NB // 2)],
                 y_send.at[k], y_recv.at[k, 2], ydev(1)).start()

        def down():
            arrived(dest.at[1], y_send.at[k], y_recv.at[k, 1], ydev(1))
            copy(dest.at[1, pl.ds(NB // 2, NB // 2)], dest.at[2, pl.ds(NB // 2, NB // 2)],
                 y_send.at[k], y_recv.at[k, 3], ydev(-1)).start()

        def done():
            arrived(dest.at[2, pl.ds(0, NB // 2)], y_send.at[k], y_recv.at[k, 2], ydev(-1))
            arrived(dest.at[2, pl.ds(NB // 2, NB // 2)], y_send.at[k], y_recv.at[k, 3], ydev(1))
            r = dest.at[pl.ds(0, 3)]
            copy(r, r, y_send.at[k], y_recv.at[k, 0], ydev(1)).wait_send()

        return first, up, down, done

    def coef(t, f, pr, pi):
        m = lax.rem(t * f, 4)
        cs = jnp.where(m == 0, 1.0, jnp.where(m == 2, -1.0, 0.0)).astype(F32)
        sn = jnp.where(m == 1, 1.0, jnp.where(m == 3, -1.0, 0.0)).astype(F32)
        return pr * cs - pi * sn, -(pr * sn + pi * cs)

    own_pr, own_pi = pulse[0, 0], pulse[0, 1]
    MID = PANELS // 2

    def share_first():
        cr, ci = coef(add4(yy, 2), yy, own_pr, own_pi)

        def body(g, carry):
            r = rows_of(g)
            part2[r, :] = cr * X0[0, r, :] + ci * X0[1, r, :]
            return carry

        lax.fori_loop(0, NB, body, 0)
        lo, hi = part2.at[pl.ds(0, MID)], part2.at[pl.ds(MID, MID)]
        copy(lo, half_in.at[0], y_send.at[0], y_recv.at[0, 0], ydev(1)).start()
        copy(hi, half_in.at[1], y_send.at[0], y_recv.at[0, 1], ydev(-1)).start()

    def share_second():
        crp, cip = coef(add4(yy, 1), yy, own_pr, own_pi)
        crm, cim = coef(add4(yy, 3), yy, own_pr, own_pi)
        arrived(half_in.at[0], y_send.at[0], y_recv.at[0, 0], ydev(-1))
        arrived(half_in.at[1], y_send.at[0], y_recv.at[0, 1], ydev(1))

        def body(g, carry):
            r, q = rows_of(g), rows_of(g + NB // 2)
            a, b = X0[0, r, :], X0[1, r, :]
            sendp[r, :] = crp * a + cip * b + half_in[0, r, :]
            sendm[r, :] = crm * a + cim * b
            a, b = X0[0, q, :], X0[1, q, :]
            sendp[q, :] = crp * a + cip * b
            sendm[q, :] = crm * a + cim * b + half_in[1, r, :]
            return carry

        lax.fori_loop(0, NB // 2, body, 0)
        copy(sendp, full_in.at[0], y_send.at[3], y_recv.at[0, 2], ydev(1)).start()
        copy(sendm, full_in.at[1], y_send.at[3], y_recv.at[0, 3], ydev(-1)).start()

    def share_done():
        arrived(full_in.at[0], y_send.at[3], y_recv.at[0, 2], ydev(-1))
        arrived(full_in.at[1], y_send.at[3], y_recv.at[0, 3], ydev(1))
        copy(part2, part2, y_send.at[0], y_recv.at[0, 0], ydev(1)).wait_send()
        copy(full_in, full_in, y_send.at[3], y_recv.at[0, 0], ydev(1)).wait_send()

    def apply(parity, xe, ag, plan, between):
        firsts, mixed, finish, drain = plan
        early, middle, late = mixed
        n = 0
        for i, s in enumerate(early):
            s()
            if i % 2 and n < PIECES - 1:
                n += 1
                halo_start(parity, xe, n)
        for s in middle:
            s()
        halo_wait(parity, xe)
        near_products(xe, late)
        for s in between:
            s()
        finish()
        crack_products(ag)
        drain()
        halo_drain(parity, xe)

    loads[0].wait()

    def low_front(g, carry):
        r = rows_of(g)
        put_low(X0[0, r, :], X0[1, r, :], g, xe0, ag0)
        return carry

    def low_rest(g, carry):
        r = rows_of(g)
        put_low(X0[0, r, :], X0[1, r, :], g, xe0, None)
        return carry

    lax.fori_loop(0, 4, low_front, 0)
    pl.semaphore_wait(barrier, len(peers))
    plan = gather(0, ag0)
    for s in plan[0]:
        s()
    lax.fori_loop(4, NB, low_rest, 0)
    halo_start(0, xe0, 0)
    share_first()

    prod[EDGES] = jnp.zeros((BLK, 2 * BLK), F32)
    loads[1].wait()
    loads[2].wait()
    loads[3].wait()

    apply(0, xe0, ag0, plan, (share_second,))

    def residual(g, acc, ag):
        r = rows_of(g)
        nr, ni = total_of(g)
        re = R[0, r, :] - (0.5 * X0[0, r, :] + nr)
        im = R[1, r, :] - (0.5 * X0[1, r, :] + ni)
        R[0, r, :] = re
        R[1, r, :] = im
        put_low(re, im, g, xe1, ag)
        return acc + fold(re * re + im * im)

    acc = lax.fori_loop(0, 4, lambda g, a: residual(g, a, ag1), zero8)
    plan = gather(1, ag1)
    for s in plan[0]:
        s()
    rr = lax.fori_loop(4, NB, lambda g, a: residual(g, a, None), acc)
    halo_start(1, xe1, 0)
    y_first, y_up, y_down, r_done = far_steps(1, xe1, far_r)
    y_first()
    rr = line(rr)

    apply(1, xe1, ag1, plan, (y_up, y_down))

    def image(g, acc, ag):
        r = rows_of(g)
        nr, ni = total_of(g)
        vr, vi = R[0, r, :], R[1, r, :]
        wr, wi = 0.5 * vr + nr, 0.5 * vi + ni
        W[0, r, :] = wr
        W[1, r, :] = wi
        put_low(wr, wi, g, xe0, ag)
        return acc[0] + fold(vr * wr + vi * wi), acc[1] + fold(vr * wi - vi * wr)

    acc = lax.fori_loop(0, 4, lambda g, a: image(g, a, ag0), (zero8,) * 2)
    plan = gather(0, ag0)
    for s in plan[0]:
        s()
    pr, pi = lax.fori_loop(4, NB, lambda g, a: image(g, a, None), acc)
    halo_start(0, xe0, 0)
    sum_cols, sum_end = clu_sum(0, [rr, line(pr), line(pi)])
    y_first, y_up, y_down, w_done = far_steps(2, xe0, far_w)
    y_first()

    apply(0, xe0, ag0, plan, (y_up, y_down, sum_cols))
    rr, pr, pi = sum_end()
    beta2 = rr + EPS
    h11r, h11i = pr / beta2, pi / beta2

    def heights(g, acc):
        r = rows_of(g)
        nr, ni = total_of(g)
        vr, vi, wr, wi = R[0, r, :], R[1, r, :], W[0, r, :], W[1, r, :]
        ur = 0.5 * wr + nr - (h11r * wr - h11i * wi)
        ui = 0.5 * wi + ni - (h11r * wi + h11i * wr)
        wr, wi = wr - (h11r * vr - h11i * vi), wi - (h11r * vi + h11i * vr)
        W[0, r, :] = wr
        W[1, r, :] = wi
        new = (wr * wr + wi * wi, vr * wr + vi * wi, vr * wi - vi * wr,
               vr * ur + vi * ui, vr * ui - vi * ur, wr * ur + wi * ui, wr * ui - wi * ur, ur * ur + ui * ui)
        return tuple(a + fold(n) for a, n in zip(acc, new))

    sums = lax.fori_loop(0, NB, heights, (zero8,) * 8)
    sum_cols, sum_end = clu_sum(1, [line(v) for v in sums])
    sum_cols()
    ww, gr, gi, ar, ai, br, bi, uu = sum_end()

    beta = jnp.sqrt(beta2)
    inv_b = 1.0 / beta
    h21 = jnp.sqrt(ww / beta2 + EPS)
    scale2 = inv_b / h21
    n1, n2 = rr * (inv_b * inv_b), ww * (scale2 * scale2)
    cross = inv_b * scale2
    h12r, h12i, g12r, g12i = ar * cross, ai * cross, gr * cross, gi * cross
    sq2 = scale2 * scale2
    h22r, h22i, un = br * sq2, bi * sq2, uu * sq2
    m12, m22 = h12r * h12r + h12i * h12i, h22r * h22r + h22i * h22i
    mixr, mixi = h12r * h22r + h12i * h22i, h12r * h22i - h12i * h22r
    rest = un + m12 * (n1 - 2.0) + m22 * (n2 - 2.0) + 2.0 * (mixr * g12r - mixi * g12i)
    h32 = jnp.sqrt(jnp.maximum(rest, 0.0) + EPS)

    r_one = jnp.sqrt(h11r * h11r + h11i * h11i + h21 * h21)
    q_real, q_imag, q_low = h11r / r_one, h11i / r_one, h21 / r_one
    mix_real = q_real * h12r + q_imag * h12i + q_low * h22r
    mix_imag = q_real * h12i - q_imag * h12r + q_low * h22i
    top_real = h12r - (mix_real * q_real - mix_imag * q_imag)
    top_imag = h12i - (mix_real * q_imag + mix_imag * q_real)
    mid_real, mid_imag = h22r - mix_real * q_low, h22i - mix_imag * q_low
    r_two_sq = top_real**2 + top_imag**2 + mid_real**2 + mid_imag**2 + h32 * h32
    y2r, y2i = beta * top_real / r_two_sq, -beta * top_imag / r_two_sq
    y1r = (beta * q_real - (mix_real * y2r - mix_imag * y2i)) / r_one
    y1i = (-beta * q_imag - (mix_real * y2i + mix_imag * y2r)) / r_one
    a1r, a1i, a2r, a2i = y1r * inv_b, y1i * inv_b, y2r * scale2, y2i * scale2

    ones = jnp.ones((1, BLK), F32)
    blank = jnp.zeros((1, BLK), F32)
    b1r, b1i = a1r - (a2r * h11r - a2i * h11i), a1i - (a2r * h11i + a2i * h11r)
    gbuf[yy] = jnp.concatenate([b1r, b1i, a2r, a2i, own_pr * ones, own_pi * ones, blank, blank], axis=0)
    for d in (1, 2, 3):
        copy(gbuf.at[yy], gbuf.at[yy], g_send.at[0], g_recv.at[0], ydev(d)).start()

    def solve(g, carry):
        r = rows_of(g)
        vr, vi, wr, wi = R[0, r, :], R[1, r, :], W[0, r, :], W[1, r, :]
        X0[0, r, :] = X0[0, r, :] + (a1r * vr - a1i * vi) + (a2r * wr - a2i * wi)
        X0[1, r, :] = X0[1, r, :] + (a1r * vi + a1i * vr) + (a2r * wi + a2i * wr)
        return carry

    lax.fori_loop(0, NB, solve, 0)
    out_scat = pltpu.make_async_copy(X0, scat_hbm, out_sem.at[0])
    out_scat.start()
    share_done()
    r_done()
    w_done()
    three = gbuf.at[pl.ds(0, 3)]
    copy(three, three, g_send.at[0], g_recv.at[0], ydev(1)).wait()

    own_cr, own_ci = coef(yy, yy, own_pr, own_pi)
    factors = []
    for d in (-1, 1, 2):
        f = add4(yy, d)
        b = gbuf[f]
        cr, ci = coef(yy, f, b[4:5, :], b[5:6, :])
        for k in (0, 2):
            er, ei = b[k:k + 1, :], b[k + 1:k + 2, :]
            factors.append((cr * er + ci * ei, ci * er - cr * ei))

    def trace(g, carry):
        r = rows_of(g)
        t = full_in[0, r, :] + full_in[1, r, :] + (own_cr * X0[0, r, :] + own_ci * X0[1, r, :])
        for i in range(3):
            for k, store in enumerate((far_r, far_w)):
                v = store[i, g].astype(F32)
                fr, fi = factors[2 * i + k]
                t = t + (fr * v[:, :BLK] + fi * v[:, BLK:])
        part2[r, :] = t
        return carry

    lax.fori_loop(0, NB, trace, 0)
    out_trace = pltpu.make_async_copy(part2, trace_hbm, out_sem.at[1])
    out_trace.start()
    out_scat.wait()
    out_trace.wait()


def local(incident, initial, near_blocks, near_pattern, crack_blocks, crack_cluster, crack_source, crack_target, pulse):
    vmem, dma = pltpu.VMEM, pltpu.SemaphoreType.DMA
    hbm, smem = pl.BlockSpec(memory_space=pl.ANY), pl.BlockSpec(memory_space=pltpu.SMEM)
    vec = (2, PANELS, BLK)
    scratch = [
        vmem((NB * NEAR, 2 * BLK, BLK), BF16),
        vmem((EDGES, 2 * BLK, BLK), BF16),
        vmem(vec, F32), vmem(vec, F32), vmem(vec, F32), vmem(vec, F32),
        vmem((EDGES + 1, BLK, 2 * BLK), F32),
        vmem((3 * NB, BLK, 2 * BLK), BF16), vmem((3 * NB, BLK, 2 * BLK), BF16),
        vmem((32 * SET, HALF, 2 * BLK), BF16), vmem((32 * SET, HALF, 2 * BLK), BF16),
        vmem((PANELS, BLK), F32), vmem((PANELS, BLK), F32), vmem((PANELS, BLK), F32),
        vmem((2, PANELS // 2, BLK), F32), vmem((2, PANELS, BLK), F32),
        vmem((3, NB, BLK, 2 * BLK), BF16), vmem((3, NB, BLK, 2 * BLK), BF16),
        vmem((2, 8, 8, BLK), F32), vmem((2, 4, 8, BLK), F32), vmem((4, 8, BLK), F32),
        dma((4,)), dma((2,)), dma((2, 44)), dma((2,)), dma((2,)), dma((2, 2)), dma((2,)),
        dma((3, 4)), dma((4,)), dma((2,)), dma((2,)), dma((2,)), dma((2,)), dma((1,)), dma((1,)),
    ]
    place = jnp.arange(EDGES + NB, dtype=I32)
    target = jnp.where(place < EDGES, jnp.pad(crack_target, (0, NB)), place - EDGES)
    each = jnp.arange(EDGES, dtype=I32)
    found = (crack_target[None, :] == target[:, None]) & (each[None, :] < place[:, None])
    links = jnp.max(jnp.where(found, each[None, :], -1), axis=1)
    links = jnp.where(links < 0, EDGES, links)
    scattered, trace = pl.pallas_call(
        kernel,
        out_shape=(jax.ShapeDtypeStruct(vec, F32), jax.ShapeDtypeStruct((PANELS, BLK), F32)),
        in_specs=[smem] * 5 + [hbm] * 4,
        out_specs=(hbm, hbm),
        scratch_shapes=scratch,
        compiler_params=pltpu.CompilerParams(
            collective_id=0, has_side_effects=True, vmem_limit_bytes=66_000_000),
        name="gmres",
    )(
        near_pattern.T, crack_cluster.T, crack_source, links, pulse,
        incident.reshape(vec), initial.reshape(vec),
        near_blocks.reshape(NB * NEAR, 2 * BLK, BLK), crack_blocks.reshape(EDGES, 2 * BLK, BLK),
    )
    return scattered[None], trace[None]


def solution(mesh):
    in_specs = (
        P("frq", None, "clu", None),
        P("frq", None, "clu", None),
        P("clu", None, "frq", None, None, None),
        P("clu", None),
        P("clu", "frq", None, None, None),
        P("clu", None),
        P("clu"),
        P("clu"),
        P("frq", None),
    )
    out_specs = (P("frq", None, "clu", None), P("frq", "clu", None))
    return jax.shard_map(local, mesh=mesh, in_specs=in_specs, out_specs=out_specs, check_vma=False)
```

```python
import functools

import jax
import jax.numpy as jnp
from jax import lax
from jax.experimental import pallas as pl
from jax.experimental.pallas import tpu as pltpu
from jax.sharding import PartitionSpec as P

MESH = pl.DeviceIdType.MESH
F32, BF16, I32 = jnp.float32, jnp.bfloat16, jnp.int32
EPS = 1e-06
BLK = 128
NB = 16
NEAR = 8
EDGES = 32
HALF = BLK // 2
SET = 8
SPAN = 2 * NB
PANELS = NB * BLK
NX = NZ = NY = 4
PIECES = 3
MIDWAY = 12
SPLIT = 4


def add4(a, d):
    return lax.rem(a + (d % 4), 4)


def kernel(
    pat, ccl, csrc, links, pulse, inc_hbm, ini_hbm, near_hbm, crack_hbm,
    scat_hbm, trace_hbm,
    A, C, R, X0, W, Y, prod, xe0, xe1, ag0, ag1,
    part2, sendp, sendm, half_in, full_in, far_r, far_w, fine, far_f,
    rowbuf, colbuf, gbuf, allbuf,
    load_sem, out_sem, ag_recv, ag_send, pair_recv, halo_recv, halo_send,
    y_recv, y_send, row_recv, row_send, col_recv, col_send, g_recv, g_send,
):
    me, yy = lax.axis_index("clu"), lax.axis_index("frq")
    core, xx = lax.rem(me, 2), lax.rem(lax.div(me, 2), 4)
    zz = lax.div(me, 8)
    spot = lax.rem(me, 8)

    def clu(dx, dz):
        return (add4(zz, dz) * 4 + add4(xx, dx)) * 2 + core

    partner = me + 1 - 2 * core
    beyond = lax.rem(me + jnp.where(core == 1, 30, 2), 32)
    right, left = lax.rem(me + 1, 32), lax.rem(me + 31, 32)

    def dev(c):
        return (c, yy)

    def ydev(dy):
        return (me, add4(yy, dy))

    def row_peer(i):
        return (me - spot + lax.rem(spot + i, 8), yy)

    def copy(src, dst, ssem, rsem, target):
        return pltpu.make_async_remote_copy(
            src_ref=src, dst_ref=dst, send_sem=ssem, recv_sem=rsem,
            device_id=target, device_id_type=MESH)

    def arrived(ref, ssem, rsem, source):
        copy(ref, ref, ssem, rsem, source).wait_recv()

    loads = [
        pltpu.make_async_copy(s, d, load_sem.at[i])
        for i, (s, d) in enumerate([(ini_hbm, X0), (near_hbm, A), (inc_hbm, R), (crack_hbm, C)])
    ]
    for l in loads:
        l.start()
    barrier = pltpu.get_barrier_semaphore()
    peers = [dev(lax.rem(me + i, 32)) for i in range(1, 32)]
    peers += [ydev(d) for d in (1, 2, 3)]
    for p in peers:
        pl.semaphore_signal(barrier, inc=1, device_id=p, device_id_type=MESH)

    def rows_of(g):
        return pl.ds(pl.multiple_of(g * BLK, BLK), BLK)

    def put_low(re, im, g, xe, ag):
        low = jnp.concatenate([re.astype(BF16), im.astype(BF16)], axis=1)
        low = low.reshape(2, HALF, 2 * BLK)
        xe[pl.ds(2 * (NB + g), 2)] = low
        if ag is not None:
            ag[pl.ds(me * SET + 2 * g, 2)] = low

    def gather_steps(parity, ag, xe, group, off, n, x_first):
        hn = n // 2
        base = 22 * group

        def at(dp, ds):
            return clu(dp, ds) if x_first else clu(ds, dp)

        def region(c, part):
            start, length = {0: (off, n), 1: (off, hn), 2: (off + hn, hn)}[part]
            return ag.at[pl.ds(c * SET + start, length)]

        def send(c, part, target, slot):
            r = region(c, part)
            copy(r, r, ag_send.at[parity], ag_recv.at[parity, base + slot], dev(target)).start()

        def wait(c, part, source, slot):
            arrived(region(c, part), ag_send.at[parity], ag_recv.at[parity, base + slot], dev(source))

        def share(c, part):
            r = region(c, part)
            copy(r, r, ag_send.at[parity], pair_recv.at[parity], dev(partner)).start()

        def to_halo(c):
            @pl.when(c == beyond)
            def _():
                there = xe.at[pl.ds(2 * SPAN * (1 - core) + off, n)]
                copy(region(c, 0), there, halo_send.at[parity], halo_recv.at[parity, 1 - core], dev(partner)).start()

        cols = [0, -1, 1]

        def first():
            send(me, 0, at(1, 0), 0)
            send(me, 0, at(-1, 0), 1)
            send(me, 0, at(0, 1), 4)
            send(me, 0, at(0, -1), 5)
            share(me, 0)

        def primary(sign):
            def step():
                c = at(-sign, 0)
                wait(c, 0, c, 0 if sign > 0 else 1)
                send(c, 1 if sign > 0 else 2, at(sign, 0), 2 if sign > 0 else 3)
                k = 1 if sign > 0 else 2
                send(c, 0, at(0, 1), 4 + 4 * k)
                send(c, 0, at(0, -1), 5 + 4 * k)
                share(c, 0)
                if x_first:
                    to_halo(c)
            return step

        def far(sign):
            def step():
                c, part = at(2, 0), 1 if sign > 0 else 2
                wait(c, part, at(-sign, 0), 2 if sign > 0 else 3)
                slot = 16 if sign > 0 else 18
                send(c, part, at(0, 1), slot)
                send(c, part, at(0, -1), slot + 1)
                share(c, part)
            return step

        def second(k, sign):
            def step():
                c = at(cols[k], -sign)
                wait(c, 0, at(0, -sign), 4 + 4 * k + (0 if sign > 0 else 1))
                send(c, 1 if sign > 0 else 2, at(0, sign), 6 + 4 * k + (0 if sign > 0 else 1))
                share(c, 0)
                if (k == 0 and not x_first) or (k, sign) in ((1, 1), (2, -1)):
                    to_halo(c)
            return step

        def second_far(part, sign):
            def step():
                c = at(2, -sign)
                slot = 16 if part == 1 else 18
                wait(c, part, at(0, -sign), slot + (0 if sign > 0 else 1))
                if (part == 1) == (sign > 0):
                    send(c, part, at(0, sign), 20 if sign > 0 else 21)
                share(c, part)
            return step

        def final(k, sign):
            def step():
                c, part = at(2 if k == 3 else cols[k], 2), 1 if sign > 0 else 2
                slot = (20 if k == 3 else 6 + 4 * k) + (0 if sign > 0 else 1)
                wait(c, part, at(0, -sign), slot)
                share(c, part)
            return step

        early = [primary(1), primary(-1)]
        early += [second(0, 1), second(0, -1)]
        middle = [second(1, 1), second(1, -1), second(2, 1), second(2, -1), far(1), far(-1)]
        middle += [second_far(1, 1), second_far(2, -1)]
        late = [second_far(1, -1), second_far(2, 1)]
        late += [final(k, s) for k in range(4) for s in (1, -1)]
        return first, early, middle, late

    def gather(parity, ag, xe):
        groups = [(0, SPLIT, True), (SPLIT, SET - SPLIT, False)]
        made = [gather_steps(parity, ag, xe, i, *g) for i, g in enumerate(groups) if g[1]]
        firsts = [m[0] for m in made]
        mixed = [[s for steps in zip(*[m[k] for m in made]) for s in steps] for k in (1, 2, 3)]
        total = 0
        for _, n, _ in groups:
            total += 15 * n + 16 * n

        def finish():
            arrived(ag.at[pl.ds(0, 16 * SET)], ag_send.at[parity], pair_recv.at[parity], dev(partner))

        def drain():
            r = ag.at[pl.ds(0, total)]
            copy(r, r, ag_send.at[parity], pair_recv.at[parity], dev(partner)).wait_send()

        return firsts, mixed, finish, drain

    def halo_start(parity, xe, piece):
        size = (SPAN - SET) // PIECES
        first = SET + piece * size
        own = xe.at[pl.ds(SPAN + first, size)]
        for k, target in ((0, right), (1, left)):
            there = xe.at[pl.ds(2 * SPAN * k + first, size)]
            copy(own, there, halo_send.at[parity], halo_recv.at[parity, k], dev(target)).start()

    def halo_fronts(parity, xe):
        there = xe.at[pl.ds(2 * SPAN * core, SET)]
        copy(xe.at[pl.ds(SPAN, SET)], there, halo_send.at[parity], halo_recv.at[parity, core], dev(partner)).start()

    def halo_wait(parity, xe):
        for k, source in ((0, left), (1, right)):
            arrived(xe.at[pl.ds(2 * SPAN * k, SPAN)], halo_send.at[parity], halo_recv.at[parity, k], dev(source))

    def halo_drain(parity, xe):
        r = xe.at[pl.ds(0, 2 * SPAN)]
        copy(r, r, halo_send.at[parity], halo_recv.at[parity, 0], dev(right)).wait_send()

    def near_products(xe, steps):
        places = {}
        for i, s in enumerate(steps):
            places.setdefault(i * NB // len(steps), []).append(s)

        def row(g, carry):
            for k, todo in places.items():
                @pl.when(g == k)
                def _(todo=todo):
                    for s in todo:
                        s()
            acc = None
            for p in range(NEAR // 2):
                a, b = 2 * pat[2 * p, g], 2 * pat[2 * p + 1, g]
                xs = jnp.concatenate([xe[a], xe[a + 1], xe[b], xe[b + 1]], axis=0)
                ms = jnp.concatenate([A[g * NEAR + 2 * p], A[g * NEAR + 2 * p + 1]], axis=1)
                d = jnp.dot(ms, xs, preferred_element_type=F32)
                acc = d if acc is None else acc + d
            r = rows_of(g)
            Y[0, r, :] = acc[:BLK, :BLK] - acc[BLK:, BLK:]
            Y[1, r, :] = acc[:BLK, BLK:] + acc[BLK:, :BLK]
            return carry

        lax.fori_loop(0, NB, row, 0)

    def crack_products(ag):
        def edge(e, carry):
            q = ccl[0, e] * 4 + csrc[e]
            xc = jnp.concatenate([ag[2 * q], ag[2 * q + 1]], axis=0)
            turned = jnp.concatenate([-xc[:, BLK:], xc[:, :BLK]], axis=1)
            xs = jnp.concatenate([xc, turned], axis=0)
            ms = jnp.concatenate([C[e, :BLK, :], C[e, BLK:, :]], axis=1)
            prod[e] = jnp.dot(ms, xs, preferred_element_type=F32) + prod[links[e]]
            return carry

        lax.fori_loop(0, EDGES, edge, 0, unroll=8)

    def total_of(g):
        r = rows_of(g)
        d = prod[links[EDGES + g]]
        return Y[0, r, :] + d[:, :BLK], Y[1, r, :] + d[:, BLK:]

    def fold(v):
        return jnp.sum(v.reshape(BLK // 8, 8, BLK), axis=0)

    zero8 = jnp.zeros((8, BLK), F32)

    def line(v):
        return jnp.sum(v, axis=0, keepdims=True)

    def clu_sum(k, lines):
        pad = [jnp.zeros((1, BLK), F32)] * (8 - len(lines))
        rowbuf[k, spot] = jnp.concatenate(lines + pad, axis=0)
        for i in range(1, 8):
            copy(rowbuf.at[k, spot], rowbuf.at[k, spot], row_send.at[k], row_recv.at[k], row_peer(i)).start()

        def cols():
            seven = rowbuf.at[k, pl.ds(0, 7)]
            copy(seven, seven, row_send.at[k], row_recv.at[k], row_peer(1)).wait()
            s = rowbuf[k, 0]
            for i in range(1, 8):
                s = s + rowbuf[k, i]
            colbuf[k, zz] = s
            for d in (1, 2, 3):
                copy(colbuf.at[k, zz], colbuf.at[k, zz], col_send.at[k], col_recv.at[k], dev(clu(0, d))).start()

        def end():
            three = colbuf.at[k, pl.ds(0, 3)]
            copy(three, three, col_send.at[k], col_recv.at[k], dev(clu(0, 1))).wait()
            s = (colbuf[k, 0] + colbuf[k, 1]) + (colbuf[k, 2] + colbuf[k, 3])
            return [s[i:i + 1, :] for i in range(len(lines))]

        return cols, end

    def far_steps(k, xe, dest):
        own = xe.at[pl.ds(SPAN, SPAN)]

        def first():
            copy(own, dest.at[0], y_send.at[k], y_recv.at[k, 0], ydev(1)).start()
            copy(own, dest.at[1], y_send.at[k], y_recv.at[k, 1], ydev(-1)).start()

        def up():
            arrived(dest.at[0], y_send.at[k], y_recv.at[k, 0], ydev(-1))
            copy(dest.at[0, pl.ds(0, NB)], dest.at[2, pl.ds(0, NB)],
                 y_send.at[k], y_recv.at[k, 2], ydev(1)).start()

        def down():
            arrived(dest.at[1], y_send.at[k], y_recv.at[k, 1], ydev(1))
            copy(dest.at[1, pl.ds(NB, NB)], dest.at[2, pl.ds(NB, NB)],
                 y_send.at[k], y_recv.at[k, 3], ydev(-1)).start()

        def done():
            arrived(dest.at[2, pl.ds(0, NB)], y_send.at[k], y_recv.at[k, 2], ydev(-1))
            arrived(dest.at[2, pl.ds(NB, NB)], y_send.at[k], y_recv.at[k, 3], ydev(1))
            r = dest.at[pl.ds(0, 3)]
            copy(r, r, y_send.at[k], y_recv.at[k, 0], ydev(1)).wait_send()

        return first, up, down, done

    def coef(t, f, pr, pi):
        m = lax.rem(t * f, 4)
        cs = jnp.where(m == 0, 1.0, jnp.where(m == 2, -1.0, 0.0)).astype(F32)
        sn = jnp.where(m == 1, 1.0, jnp.where(m == 3, -1.0, 0.0)).astype(F32)
        return pr * cs - pi * sn, -(pr * sn + pi * cs)

    own_pr, own_pi = pulse[0, 0], pulse[0, 1]
    MID = PANELS // 2

    def share_first():
        cr, ci = coef(add4(yy, 2), yy, own_pr, own_pi)

        def body(g, carry):
            r = rows_of(g)
            part2[r, :] = cr * X0[0, r, :] + ci * X0[1, r, :]
            return carry

        lax.fori_loop(0, NB, body, 0)
        lo, hi = part2.at[pl.ds(0, MID)], part2.at[pl.ds(MID, MID)]
        copy(lo, half_in.at[0], y_send.at[0], y_recv.at[0, 0], ydev(1)).start()
        copy(hi, half_in.at[1], y_send.at[0], y_recv.at[0, 1], ydev(-1)).start()

    def share_second():
        crp, cip = coef(add4(yy, 1), yy, own_pr, own_pi)
        crm, cim = coef(add4(yy, 3), yy, own_pr, own_pi)
        arrived(half_in.at[0], y_send.at[0], y_recv.at[0, 0], ydev(-1))
        arrived(half_in.at[1], y_send.at[0], y_recv.at[0, 1], ydev(1))

        def body(g, carry):
            r, q = rows_of(g), rows_of(g + NB // 2)
            a, b = X0[0, r, :], X0[1, r, :]
            sendp[r, :] = crp * a + cip * b + half_in[0, r, :]
            sendm[r, :] = crm * a + cim * b
            a, b = X0[0, q, :], X0[1, q, :]
            sendp[q, :] = crp * a + cip * b
            sendm[q, :] = crm * a + cim * b + half_in[1, r, :]
            return carry

        lax.fori_loop(0, NB // 2, body, 0)
        copy(sendp, full_in.at[0], y_send.at[4], y_recv.at[0, 2], ydev(1)).start()
        copy(sendm, full_in.at[1], y_send.at[4], y_recv.at[0, 3], ydev(-1)).start()

    def share_done():
        arrived(full_in.at[0], y_send.at[4], y_recv.at[0, 2], ydev(-1))
        arrived(full_in.at[1], y_send.at[4], y_recv.at[0, 3], ydev(1))
        copy(part2, part2, y_send.at[0], y_recv.at[0, 0], ydev(1)).wait_send()
        copy(full_in, full_in, y_send.at[4], y_recv.at[0, 0], ydev(1)).wait_send()

    def apply(parity, xe, ag, plan, mid, between):
        firsts, mixed, finish, drain = plan
        early, middle, late = mixed
        n = 0
        for i, s in enumerate(early):
            s()
            if i % 2 and n < PIECES - 1:
                n += 1
                halo_start(parity, xe, n)
        for s in middle[:MIDWAY] + list(mid) + middle[MIDWAY:]:
            s()
        halo_wait(parity, xe)
        near_products(xe, late)
        for s in between:
            s()
        finish()
        crack_products(ag)
        drain()
        halo_drain(parity, xe)

    loads[0].wait()

    def low_front(g, carry):
        r = rows_of(g)
        put_low(X0[0, r, :], X0[1, r, :], g, xe0, ag0)
        return carry

    def low_rest(g, carry):
        r = rows_of(g)
        put_low(X0[0, r, :], X0[1, r, :], g, xe0, None)
        return carry

    lax.fori_loop(0, 4, low_front, 0)
    pl.semaphore_wait(barrier, len(peers))
    plan = gather(0, ag0, xe0)
    for s in plan[0]:
        s()
    lax.fori_loop(4, NB, low_rest, 0)
    halo_fronts(0, xe0)
    halo_start(0, xe0, 0)
    share_first()

    prod[EDGES] = jnp.zeros((BLK, 2 * BLK), F32)
    loads[1].wait()
    loads[2].wait()
    loads[3].wait()

    apply(0, xe0, ag0, plan, (share_second,), ())

    def residual(g, acc, ag):
        r = rows_of(g)
        nr, ni = total_of(g)
        re = R[0, r, :] - (0.5 * X0[0, r, :] + nr)
        im = R[1, r, :] - (0.5 * X0[1, r, :] + ni)
        R[0, r, :] = re
        R[1, r, :] = im
        put_low(re, im, g, xe1, ag)
        less = [(v - v.astype(BF16).astype(F32)).astype(BF16) for v in (re, im)]
        fine[pl.ds(2 * g, 2)] = jnp.concatenate(less, axis=1).reshape(2, HALF, 2 * BLK)
        return acc + fold(re * re + im * im)

    acc = lax.fori_loop(0, 4, lambda g, a: residual(g, a, ag1), zero8)
    plan = gather(1, ag1, xe1)
    for s in plan[0]:
        s()
    rr = lax.fori_loop(4, NB, lambda g, a: residual(g, a, None), acc)
    halo_fronts(1, xe1)
    halo_start(1, xe1, 0)
    y_first, y_up, y_down, r_done = far_steps(1, xe1, far_r)
    y_first()
    lo, hi = pl.ds(0, NB), pl.ds(NB, NB)
    copy(fine.at[lo], far_f.at[lo], y_send.at[3], y_recv.at[3, 0], ydev(1)).start()
    copy(fine.at[hi], far_f.at[hi], y_send.at[3], y_recv.at[3, 1], ydev(-1)).start()

    def fine_done():
        arrived(far_f.at[lo], y_send.at[3], y_recv.at[3, 0], ydev(-1))
        arrived(far_f.at[hi], y_send.at[3], y_recv.at[3, 1], ydev(1))
        copy(far_f, far_f, y_send.at[3], y_recv.at[3, 0], ydev(1)).wait_send()

    rr = line(rr)
    apply(1, xe1, ag1, plan, (), (y_up, y_down))

    def image(g, acc, ag):
        r = rows_of(g)
        nr, ni = total_of(g)
        vr, vi = R[0, r, :], R[1, r, :]
        wr, wi = 0.5 * vr + nr, 0.5 * vi + ni
        W[0, r, :] = wr
        W[1, r, :] = wi
        put_low(wr, wi, g, xe0, ag)
        return acc[0] + fold(vr * wr + vi * wi), acc[1] + fold(vr * wi - vi * wr)

    acc = lax.fori_loop(0, 4, lambda g, a: image(g, a, ag0), (zero8,) * 2)
    plan = gather(0, ag0, xe0)
    for s in plan[0]:
        s()
    pr, pi = lax.fori_loop(4, NB, lambda g, a: image(g, a, None), acc)
    halo_fronts(0, xe0)
    halo_start(0, xe0, 0)
    sum_cols, sum_end = clu_sum(0, [rr, line(pr), line(pi)])
    y_first, y_up, y_down, w_done = far_steps(2, xe0, far_w)
    y_first()

    apply(0, xe0, ag0, plan, (), (sum_cols, y_up, y_down))
    rr, pr, pi = sum_end()
    beta2 = rr + EPS
    h11r, h11i = pr / beta2, pi / beta2

    def heights(g, acc):
        r = rows_of(g)
        nr, ni = total_of(g)
        vr, vi, wr, wi = R[0, r, :], R[1, r, :], W[0, r, :], W[1, r, :]
        ur = 0.5 * wr + nr - (h11r * wr - h11i * wi)
        ui = 0.5 * wi + ni - (h11r * wi + h11i * wr)
        wr, wi = wr - (h11r * vr - h11i * vi), wi - (h11r * vi + h11i * vr)
        W[0, r, :] = wr
        W[1, r, :] = wi
        new = (wr * wr + wi * wi, vr * wr + vi * wi, vr * wi - vi * wr,
               vr * ur + vi * ui, vr * ui - vi * ur, wr * ur + wi * ui, wr * ui - wi * ur, ur * ur + ui * ui)
        return tuple(a + fold(n) for a, n in zip(acc, new))

    sums = lax.fori_loop(0, NB, heights, (zero8,) * 8)
    allbuf[me] = jnp.concatenate([line(v) for v in sums], axis=0)
    for i in range(1, 32):
        peer = dev(lax.rem(me + i, 32))
        copy(allbuf.at[me], allbuf.at[me], col_send.at[1], col_recv.at[1], peer).start()
    rest31 = allbuf.at[pl.ds(0, 31)]
    copy(rest31, rest31, col_send.at[1], col_recv.at[1], dev(right)).wait()
    terms = [allbuf[i] for i in range(32)]
    while len(terms) > 1:
        terms = [a + b for a, b in zip(terms[::2], terms[1::2])]
    ww, gr, gi, ar, ai, br, bi, uu = [terms[0][i:i + 1, :] for i in range(8)]

    beta = jnp.sqrt(beta2)
    inv_b = 1.0 / beta
    h21 = jnp.sqrt(ww / beta2 + EPS)
    scale2 = inv_b / h21
    n1, n2 = rr * (inv_b * inv_b), ww * (scale2 * scale2)
    cross = inv_b * scale2
    h12r, h12i, g12r, g12i = ar * cross, ai * cross, gr * cross, gi * cross
    sq2 = scale2 * scale2
    h22r, h22i, un = br * sq2, bi * sq2, uu * sq2
    m12, m22 = h12r * h12r + h12i * h12i, h22r * h22r + h22i * h22i
    mixr, mixi = h12r * h22r + h12i * h22i, h12r * h22i - h12i * h22r
    rest = un + m12 * (n1 - 2.0) + m22 * (n2 - 2.0) + 2.0 * (mixr * g12r - mixi * g12i)
    h32 = jnp.sqrt(jnp.maximum(rest, 0.0) + EPS)

    r_one = jnp.sqrt(h11r * h11r + h11i * h11i + h21 * h21)
    q_real, q_imag, q_low = h11r / r_one, h11i / r_one, h21 / r_one
    mix_real = q_real * h12r + q_imag * h12i + q_low * h22r
    mix_imag = q_real * h12i - q_imag * h12r + q_low * h22i
    top_real = h12r - (mix_real * q_real - mix_imag * q_imag)
    top_imag = h12i - (mix_real * q_imag + mix_imag * q_real)
    mid_real, mid_imag = h22r - mix_real * q_low, h22i - mix_imag * q_low
    r_two_sq = top_real**2 + top_imag**2 + mid_real**2 + mid_imag**2 + h32 * h32
    y2r, y2i = beta * top_real / r_two_sq, -beta * top_imag / r_two_sq
    y1r = (beta * q_real - (mix_real * y2r - mix_imag * y2i)) / r_one
    y1i = (-beta * q_imag - (mix_real * y2i + mix_imag * y2r)) / r_one
    a1r, a1i, a2r, a2i = y1r * inv_b, y1i * inv_b, y2r * scale2, y2i * scale2

    ones = jnp.ones((1, BLK), F32)
    blank = jnp.zeros((1, BLK), F32)
    b1r, b1i = a1r - (a2r * h11r - a2i * h11i), a1i - (a2r * h11i + a2i * h11r)
    gbuf[yy] = jnp.concatenate([b1r, b1i, a2r, a2i, own_pr * ones, own_pi * ones, blank, blank], axis=0)
    for d in (1, 2, 3):
        copy(gbuf.at[yy], gbuf.at[yy], g_send.at[0], g_recv.at[0], ydev(d)).start()

    def solve(g, carry):
        r = rows_of(g)
        vr, vi, wr, wi = R[0, r, :], R[1, r, :], W[0, r, :], W[1, r, :]
        X0[0, r, :] = X0[0, r, :] + (a1r * vr - a1i * vi) + (a2r * wr - a2i * wi)
        X0[1, r, :] = X0[1, r, :] + (a1r * vi + a1i * vr) + (a2r * wi + a2i * wr)
        return carry

    lax.fori_loop(0, NB, solve, 0)
    out_scat = pltpu.make_async_copy(X0, scat_hbm, out_sem.at[0])
    out_scat.start()
    share_done()
    r_done()
    fine_done()
    w_done()
    three = gbuf.at[pl.ds(0, 3)]
    copy(three, three, g_send.at[0], g_recv.at[0], ydev(1)).wait()

    own_cr, own_ci = coef(yy, yy, own_pr, own_pi)
    factors = []
    for d in (-1, 1, 2):
        f = add4(yy, d)
        b = gbuf[f]
        cr, ci = coef(yy, f, b[4:5, :], b[5:6, :])
        for k in (0, 2):
            er, ei = b[k:k + 1, :], b[k + 1:k + 2, :]
            factors.append((cr * er + ci * ei, ci * er - cr * ei))

    def load_block(store, g):
        return store[pl.ds(2 * g, 2)].reshape(BLK, 2 * BLK).astype(F32)

    def trace(g, nearest):
        r = rows_of(g)
        t = full_in[0, r, :] + full_in[1, r, :] + (own_cr * X0[0, r, :] + own_ci * X0[1, r, :])
        for i in range(3):
            for k, store in enumerate((far_r, far_w)):
                v = load_block(store.at[i], g)
                if k == 0 and i == nearest:
                    v = v + load_block(far_f, g)
                fr, fi = factors[2 * i + k]
                t = t + (fr * v[:, :BLK] + fi * v[:, BLK:])
        part2[r, :] = t
        return 0

    lax.fori_loop(0, NB // 2, lambda g, _: trace(g, 0), 0)
    lax.fori_loop(NB // 2, NB, lambda g, _: trace(g, 1), 0)
    out_trace = pltpu.make_async_copy(part2, trace_hbm, out_sem.at[1])
    out_trace.start()
    out_scat.wait()
    out_trace.wait()


def local(incident, initial, near_blocks, near_pattern, crack_blocks, crack_cluster, crack_source, crack_target, pulse):
    vmem, dma = pltpu.VMEM, pltpu.SemaphoreType.DMA
    hbm, smem = pl.BlockSpec(memory_space=pl.ANY), pl.BlockSpec(memory_space=pltpu.SMEM)
    vec = (2, PANELS, BLK)
    scratch = [
        vmem((NB * NEAR, 2 * BLK, BLK), BF16),
        vmem((EDGES, 2 * BLK, BLK), BF16),
        vmem(vec, F32), vmem(vec, F32), vmem(vec, F32), vmem(vec, F32),
        vmem((EDGES + 1, BLK, 2 * BLK), F32),
        vmem((3 * SPAN, HALF, 2 * BLK), BF16), vmem((3 * SPAN, HALF, 2 * BLK), BF16),
        vmem((32 * SET, HALF, 2 * BLK), BF16), vmem((32 * SET, HALF, 2 * BLK), BF16),
        vmem((PANELS, BLK), F32), vmem((PANELS, BLK), F32), vmem((PANELS, BLK), F32),
        vmem((2, PANELS // 2, BLK), F32), vmem((2, PANELS, BLK), F32),
        vmem((3, SPAN, HALF, 2 * BLK), BF16), vmem((3, SPAN, HALF, 2 * BLK), BF16),
        vmem((SPAN, HALF, 2 * BLK), BF16), vmem((SPAN, HALF, 2 * BLK), BF16),
        vmem((1, 8, 8, BLK), F32), vmem((1, 4, 8, BLK), F32), vmem((4, 8, BLK), F32), vmem((32, 8, BLK), F32),
        dma((4,)), dma((2,)), dma((2, 44)), dma((2,)), dma((2,)), dma((2, 2)), dma((2,)),
        dma((4, 4)), dma((5,)), dma((2,)), dma((2,)), dma((2,)), dma((2,)), dma((1,)), dma((1,)),
    ]
    place = jnp.arange(EDGES + NB, dtype=I32)
    target = jnp.where(place < EDGES, jnp.pad(crack_target, (0, NB)), place - EDGES)
    each = jnp.arange(EDGES, dtype=I32)
    found = (crack_target[None, :] == target[:, None]) & (each[None, :] < place[:, None])
    links = jnp.max(jnp.where(found, each[None, :], -1), axis=1)
    links = jnp.where(links < 0, EDGES, links)
    scattered, trace = pl.pallas_call(
        kernel,
        out_shape=(jax.ShapeDtypeStruct(vec, F32), jax.ShapeDtypeStruct((PANELS, BLK), F32)),
        in_specs=[smem] * 5 + [hbm] * 4,
        out_specs=(hbm, hbm),
        scratch_shapes=scratch,
        compiler_params=pltpu.CompilerParams(
            collective_id=0, has_side_effects=True, vmem_limit_bytes=66_000_000),
        name="gmres",
    )(
        near_pattern.T, crack_cluster.T, crack_source, links, pulse,
        incident.reshape(vec), initial.reshape(vec),
        near_blocks.reshape(NB * NEAR, 2 * BLK, BLK), crack_blocks.reshape(EDGES, 2 * BLK, BLK),
    )
    return scattered[None], trace[None]


def solution(mesh):
    in_specs = (
        P("frq", None, "clu", None),
        P("frq", None, "clu", None),
        P("clu", None, "frq", None, None, None),
        P("clu", None),
        P("clu", "frq", None, None, None),
        P("clu", None),
        P("clu"),
        P("clu"),
        P("frq", None),
    )
    out_specs = (P("frq", None, "clu", None), P("frq", "clu", None))
    return jax.shard_map(local, mesh=mesh, in_specs=in_specs, out_specs=out_specs, check_vma=False)
```

```python
import functools

import jax
import jax.numpy as jnp
from jax import lax
from jax.experimental import pallas as pl
from jax.experimental.pallas import tpu as pltpu
from jax.sharding import PartitionSpec as P

MESH = pl.DeviceIdType.MESH
F32, BF16, I32 = jnp.float32, jnp.bfloat16, jnp.int32
EPS = 1e-06
BLK = 128
NB = 16
NEAR = 8
EDGES = 32
HALF = BLK // 2
SET = 8
SPAN = 2 * NB
PANELS = NB * BLK
NX = NZ = NY = 4
PIECES = 3
MIDWAY = 12
SPLIT = 4


def add4(a, d):
    return lax.rem(a + (d % 4), 4)


def kernel(
    pat, ccl, csrc, links, pulse, inc_hbm, ini_hbm, near_hbm, crack_hbm,
    scat_hbm, trace_hbm,
    A, C, R, X0, W, Y, prod, xe0, xe1, ag0, ag1,
    part2, sendp, sendm, half_in, full_in, far_r, far_w, fine, far_f,
    rowbuf, colbuf, gbuf, allbuf,
    load_sem, out_sem, ag_recv, ag_send, pair_recv, halo_recv, halo_send,
    y_recv, y_send, row_recv, row_send, col_recv, col_send, g_recv, g_send,
):
    me, yy = lax.axis_index("clu"), lax.axis_index("frq")
    core, xx = lax.rem(me, 2), lax.rem(lax.div(me, 2), 4)
    zz = lax.div(me, 8)
    spot = lax.rem(me, 8)

    def clu(dx, dz):
        return (add4(zz, dz) * 4 + add4(xx, dx)) * 2 + core

    partner = me + 1 - 2 * core
    beyond = lax.rem(me + jnp.where(core == 1, 30, 2), 32)
    right, left = lax.rem(me + 1, 32), lax.rem(me + 31, 32)

    def dev(c):
        return (c, yy)

    def ydev(dy):
        return (me, add4(yy, dy))

    def row_peer(i):
        return (me - spot + lax.rem(spot + i, 8), yy)

    def copy(src, dst, ssem, rsem, target):
        return pltpu.make_async_remote_copy(
            src_ref=src, dst_ref=dst, send_sem=ssem, recv_sem=rsem,
            device_id=target, device_id_type=MESH)

    def arrived(ref, ssem, rsem, source):
        copy(ref, ref, ssem, rsem, source).wait_recv()

    loads = [
        pltpu.make_async_copy(s, d, load_sem.at[i])
        for i, (s, d) in enumerate([(ini_hbm, X0), (near_hbm, A), (inc_hbm, R), (crack_hbm, C)])
    ]
    for l in loads:
        l.start()
    barrier = pltpu.get_barrier_semaphore()
    peers = [dev(lax.rem(me + i, 32)) for i in range(1, 32)]
    peers += [ydev(d) for d in (1, 2, 3)]
    for p in peers:
        pl.semaphore_signal(barrier, inc=1, device_id=p, device_id_type=MESH)

    def rows_of(g):
        return pl.ds(pl.multiple_of(g * BLK, BLK), BLK)

    def put_low(re, im, g, xe, ag):
        low = jnp.concatenate([re.astype(BF16), im.astype(BF16)], axis=1)
        low = low.reshape(2, HALF, 2 * BLK)
        xe[pl.ds(2 * (NB + g), 2)] = low
        if ag is not None:
            ag[pl.ds(me * SET + 2 * g, 2)] = low

    def gather_steps(parity, ag, xe, group, off, n, x_first):
        hn = n // 2
        base = 22 * group

        def at(dp, ds):
            return clu(dp, ds) if x_first else clu(ds, dp)

        def region(c, part):
            start, length = {0: (off, n), 1: (off, hn), 2: (off + hn, hn)}[part]
            return ag.at[pl.ds(c * SET + start, length)]

        def send(c, part, target, slot):
            r = region(c, part)
            copy(r, r, ag_send.at[parity], ag_recv.at[parity, base + slot], dev(target)).start()

        def wait(c, part, source, slot):
            arrived(region(c, part), ag_send.at[parity], ag_recv.at[parity, base + slot], dev(source))

        def share(c, part):
            r = region(c, part)
            copy(r, r, ag_send.at[parity], pair_recv.at[parity], dev(partner)).start()

        def to_halo(c):
            @pl.when(c == beyond)
            def _():
                there = xe.at[pl.ds(2 * SPAN * (1 - core) + off, n)]
                copy(region(c, 0), there, halo_send.at[parity], halo_recv.at[parity, 1 - core], dev(partner)).start()

        cols = [0, -1, 1]

        def first():
            send(me, 0, at(1, 0), 0)
            send(me, 0, at(-1, 0), 1)
            send(me, 0, at(0, 1), 4)
            send(me, 0, at(0, -1), 5)
            share(me, 0)

        def primary(sign):
            def step():
                c = at(-sign, 0)
                wait(c, 0, c, 0 if sign > 0 else 1)
                send(c, 1 if sign > 0 else 2, at(sign, 0), 2 if sign > 0 else 3)
                k = 1 if sign > 0 else 2
                send(c, 0, at(0, 1), 4 + 4 * k)
                send(c, 0, at(0, -1), 5 + 4 * k)
                share(c, 0)
                if x_first:
                    to_halo(c)
            return step

        def far(sign):
            def step():
                c, part = at(2, 0), 1 if sign > 0 else 2
                wait(c, part, at(-sign, 0), 2 if sign > 0 else 3)
                slot = 16 if sign > 0 else 18
                send(c, part, at(0, 1), slot)
                send(c, part, at(0, -1), slot + 1)
                share(c, part)
            return step

        def second(k, sign):
            def step():
                c = at(cols[k], -sign)
                wait(c, 0, at(0, -sign), 4 + 4 * k + (0 if sign > 0 else 1))
                send(c, 1 if sign > 0 else 2, at(0, sign), 6 + 4 * k + (0 if sign > 0 else 1))
                share(c, 0)
                if (k == 0 and not x_first) or (k, sign) in ((1, 1), (2, -1)):
                    to_halo(c)
            return step

        def second_far(part, sign):
            def step():
                c = at(2, -sign)
                slot = 16 if part == 1 else 18
                wait(c, part, at(0, -sign), slot + (0 if sign > 0 else 1))
                if (part == 1) == (sign > 0):
                    send(c, part, at(0, sign), 20 if sign > 0 else 21)
                share(c, part)
            return step

        def final(k, sign):
            def step():
                c, part = at(2 if k == 3 else cols[k], 2), 1 if sign > 0 else 2
                slot = (20 if k == 3 else 6 + 4 * k) + (0 if sign > 0 else 1)
                wait(c, part, at(0, -sign), slot)
                share(c, part)
            return step

        early = [primary(1), primary(-1)]
        middle = [far(1), far(-1), second(0, 1), second(0, -1), second(1, 1), second(1, -1), second(2, 1), second(2, -1), second_far(1, 1), second_far(2, -1), ]
        late = [second_far(1, -1), second_far(2, 1)]
        late += [final(k, s) for k in range(4) for s in (1, -1)]
        return first, early, middle, late

    def gather(parity, ag, xe):
        groups = [(0, SPLIT, True), (SPLIT, SET - SPLIT, False)]
        made = [gather_steps(parity, ag, xe, i, *g) for i, g in enumerate(groups) if g[1]]
        firsts = [m[0] for m in made]
        mixed = [[s for steps in zip(*[m[k] for m in made]) for s in steps] for k in (1, 2, 3)]
        total = 0
        for _, n, _ in groups:
            total += 15 * n + 16 * n

        def finish():
            arrived(ag.at[pl.ds(0, 16 * SET)], ag_send.at[parity], pair_recv.at[parity], dev(partner))

        def drain():
            r = ag.at[pl.ds(0, total)]
            copy(r, r, ag_send.at[parity], pair_recv.at[parity], dev(partner)).wait_send()

        return firsts, mixed, finish, drain

    def halo_start(parity, xe, piece):
        size = (SPAN - SET) // PIECES
        first = SET + piece * size
        own = xe.at[pl.ds(SPAN + first, size)]
        for k, target in ((0, right), (1, left)):
            there = xe.at[pl.ds(2 * SPAN * k + first, size)]
            copy(own, there, halo_send.at[parity], halo_recv.at[parity, k], dev(target)).start()

    def halo_fronts(parity, xe):
        there = xe.at[pl.ds(2 * SPAN * core, SET)]
        copy(xe.at[pl.ds(SPAN, SET)], there, halo_send.at[parity], halo_recv.at[parity, core], dev(partner)).start()

    def halo_wait(parity, xe):
        for k, source in ((0, left), (1, right)):
            arrived(xe.at[pl.ds(2 * SPAN * k, SPAN)], halo_send.at[parity], halo_recv.at[parity, k], dev(source))

    def halo_drain(parity, xe):
        r = xe.at[pl.ds(0, 2 * SPAN)]
        copy(r, r, halo_send.at[parity], halo_recv.at[parity, 0], dev(right)).wait_send()

    def near_products(xe, steps):
        places = {}
        for i, s in enumerate(steps):
            places.setdefault(i * NB // len(steps), []).append(s)

        def row(g, carry):
            for k, todo in places.items():
                @pl.when(g == k)
                def _(todo=todo):
                    for s in todo:
                        s()
            acc = None
            for p in range(NEAR // 2):
                a, b = 2 * pat[2 * p, g], 2 * pat[2 * p + 1, g]
                xs = jnp.concatenate([xe[a], xe[a + 1], xe[b], xe[b + 1]], axis=0)
                ms = jnp.concatenate([A[g * NEAR + 2 * p], A[g * NEAR + 2 * p + 1]], axis=1)
                d = jnp.dot(ms, xs, preferred_element_type=F32)
                acc = d if acc is None else acc + d
            r = rows_of(g)
            Y[0, r, :] = acc[:BLK, :BLK] - acc[BLK:, BLK:]
            Y[1, r, :] = acc[:BLK, BLK:] + acc[BLK:, :BLK]
            return carry

        lax.fori_loop(0, NB, row, 0)

    def crack_products(ag):
        def edge(e, carry):
            q = ccl[0, e] * 4 + csrc[e]
            xc = jnp.concatenate([ag[2 * q], ag[2 * q + 1]], axis=0)
            turned = jnp.concatenate([-xc[:, BLK:], xc[:, :BLK]], axis=1)
            xs = jnp.concatenate([xc, turned], axis=0)
            ms = jnp.concatenate([C[e, :BLK, :], C[e, BLK:, :]], axis=1)
            prod[e] = jnp.dot(ms, xs, preferred_element_type=F32) + prod[links[e]]
            return carry

        lax.fori_loop(0, EDGES, edge, 0, unroll=8)

    def total_of(g):
        r = rows_of(g)
        d = prod[links[EDGES + g]]
        return Y[0, r, :] + d[:, :BLK], Y[1, r, :] + d[:, BLK:]

    def fold(v):
        return jnp.sum(v.reshape(BLK // 8, 8, BLK), axis=0)

    zero8 = jnp.zeros((8, BLK), F32)

    def line(v):
        return jnp.sum(v, axis=0, keepdims=True)

    def clu_sum(k, lines):
        pad = [jnp.zeros((1, BLK), F32)] * (8 - len(lines))
        rowbuf[k, spot] = jnp.concatenate(lines + pad, axis=0)
        for i in range(1, 8):
            copy(rowbuf.at[k, spot], rowbuf.at[k, spot], row_send.at[k], row_recv.at[k], row_peer(i)).start()

        def cols():
            seven = rowbuf.at[k, pl.ds(0, 7)]
            copy(seven, seven, row_send.at[k], row_recv.at[k], row_peer(1)).wait()
            s = rowbuf[k, 0]
            for i in range(1, 8):
                s = s + rowbuf[k, i]
            colbuf[k, zz] = s
            for d in (1, 2, 3):
                copy(colbuf.at[k, zz], colbuf.at[k, zz], col_send.at[k], col_recv.at[k], dev(clu(0, d))).start()

        def end():
            three = colbuf.at[k, pl.ds(0, 3)]
            copy(three, three, col_send.at[k], col_recv.at[k], dev(clu(0, 1))).wait()
            s = (colbuf[k, 0] + colbuf[k, 1]) + (colbuf[k, 2] + colbuf[k, 3])
            return [s[i:i + 1, :] for i in range(len(lines))]

        return cols, end

    def far_steps(k, xe, dest):
        own = xe.at[pl.ds(SPAN, SPAN)]

        def first():
            copy(own, dest.at[0], y_send.at[k], y_recv.at[k, 0], ydev(1)).start()
            copy(own, dest.at[1], y_send.at[k], y_recv.at[k, 1], ydev(-1)).start()

        def up():
            arrived(dest.at[0], y_send.at[k], y_recv.at[k, 0], ydev(-1))
            copy(dest.at[0, pl.ds(0, NB)], dest.at[2, pl.ds(0, NB)],
                 y_send.at[k], y_recv.at[k, 2], ydev(1)).start()

        def down():
            arrived(dest.at[1], y_send.at[k], y_recv.at[k, 1], ydev(1))
            copy(dest.at[1, pl.ds(NB, NB)], dest.at[2, pl.ds(NB, NB)],
                 y_send.at[k], y_recv.at[k, 3], ydev(-1)).start()

        def done():
            arrived(dest.at[2, pl.ds(0, NB)], y_send.at[k], y_recv.at[k, 2], ydev(-1))
            arrived(dest.at[2, pl.ds(NB, NB)], y_send.at[k], y_recv.at[k, 3], ydev(1))
            r = dest.at[pl.ds(0, 3)]
            copy(r, r, y_send.at[k], y_recv.at[k, 0], ydev(1)).wait_send()

        return first, up, down, done

    def coef(t, f, pr, pi):
        m = lax.rem(t * f, 4)
        cs = jnp.where(m == 0, 1.0, jnp.where(m == 2, -1.0, 0.0)).astype(F32)
        sn = jnp.where(m == 1, 1.0, jnp.where(m == 3, -1.0, 0.0)).astype(F32)
        return pr * cs - pi * sn, -(pr * sn + pi * cs)

    own_pr, own_pi = pulse[0, 0], pulse[0, 1]
    MID = PANELS // 2

    def share_first():
        cr, ci = coef(add4(yy, 2), yy, own_pr, own_pi)

        def body(g, carry):
            r = rows_of(g)
            part2[r, :] = cr * X0[0, r, :] + ci * X0[1, r, :]
            return carry

        lax.fori_loop(0, NB, body, 0)
        lo, hi = part2.at[pl.ds(0, MID)], part2.at[pl.ds(MID, MID)]
        copy(lo, half_in.at[0], y_send.at[0], y_recv.at[0, 0], ydev(1)).start()
        copy(hi, half_in.at[1], y_send.at[0], y_recv.at[0, 1], ydev(-1)).start()

    def share_second():
        crp, cip = coef(add4(yy, 1), yy, own_pr, own_pi)
        crm, cim = coef(add4(yy, 3), yy, own_pr, own_pi)
        arrived(half_in.at[0], y_send.at[0], y_recv.at[0, 0], ydev(-1))
        arrived(half_in.at[1], y_send.at[0], y_recv.at[0, 1], ydev(1))

        def body(g, carry):
            r, q = rows_of(g), rows_of(g + NB // 2)
            a, b = X0[0, r, :], X0[1, r, :]
            sendp[r, :] = crp * a + cip * b + half_in[0, r, :]
            sendm[r, :] = crm * a + cim * b
            a, b = X0[0, q, :], X0[1, q, :]
            sendp[q, :] = crp * a + cip * b
            sendm[q, :] = crm * a + cim * b + half_in[1, r, :]
            return carry

        lax.fori_loop(0, NB // 2, body, 0)
        copy(sendp, full_in.at[0], y_send.at[4], y_recv.at[0, 2], ydev(1)).start()
        copy(sendm, full_in.at[1], y_send.at[4], y_recv.at[0, 3], ydev(-1)).start()

    def share_done():
        arrived(full_in.at[0], y_send.at[4], y_recv.at[0, 2], ydev(-1))
        arrived(full_in.at[1], y_send.at[4], y_recv.at[0, 3], ydev(1))
        copy(part2, part2, y_send.at[0], y_recv.at[0, 0], ydev(1)).wait_send()
        copy(full_in, full_in, y_send.at[4], y_recv.at[0, 0], ydev(1)).wait_send()

    def apply(parity, xe, ag, plan, mid, between):
        firsts, mixed, finish, drain = plan
        early, middle, late = mixed
        n = 0
        for i, s in enumerate(early):
            s()
            if i % 2 and n < PIECES - 1:
                n += 1
                halo_start(parity, xe, n)
        for s in middle[:MIDWAY] + list(mid) + middle[MIDWAY:]:
            s()
        halo_wait(parity, xe)
        near_products(xe, late)
        for s in between:
            s()
        finish()
        crack_products(ag)

        def drained():
            drain()
            halo_drain(parity, xe)

        return drained

    loads[0].wait()

    def low_front(g, carry):
        r = rows_of(g)
        put_low(X0[0, r, :], X0[1, r, :], g, xe0, ag0)
        return carry

    def low_rest(g, carry):
        r = rows_of(g)
        put_low(X0[0, r, :], X0[1, r, :], g, xe0, None)
        return carry

    lax.fori_loop(0, 4, low_front, 0)
    pl.semaphore_wait(barrier, len(peers))
    plan = gather(0, ag0, xe0)
    for s in plan[0]:
        s()
    lax.fori_loop(4, NB, low_rest, 0)
    halo_fronts(0, xe0)
    halo_start(0, xe0, 0)
    share_first()

    prod[EDGES] = jnp.zeros((BLK, 2 * BLK), F32)
    loads[1].wait()
    loads[2].wait()
    loads[3].wait()

    sent = apply(0, xe0, ag0, plan, (share_second,), ())

    def residual(g, acc, ag):
        r = rows_of(g)
        nr, ni = total_of(g)
        re = R[0, r, :] - (0.5 * X0[0, r, :] + nr)
        im = R[1, r, :] - (0.5 * X0[1, r, :] + ni)
        R[0, r, :] = re
        R[1, r, :] = im
        put_low(re, im, g, xe1, ag)
        less = [(v - v.astype(BF16).astype(F32)).astype(BF16) for v in (re, im)]
        fine[pl.ds(2 * g, 2)] = jnp.concatenate(less, axis=1).reshape(2, HALF, 2 * BLK)
        return acc + fold(re * re + im * im)

    acc = lax.fori_loop(0, 4, lambda g, a: residual(g, a, ag1), zero8)
    sent()
    plan = gather(1, ag1, xe1)
    for s in plan[0]:
        s()
    rr = lax.fori_loop(4, NB, lambda g, a: residual(g, a, None), acc)
    halo_fronts(1, xe1)
    halo_start(1, xe1, 0)
    y_first, y_up, y_down, r_done = far_steps(1, xe1, far_r)
    y_first()
    lo, hi = pl.ds(0, NB), pl.ds(NB, NB)
    copy(fine.at[lo], far_f.at[lo], y_send.at[3], y_recv.at[3, 0], ydev(1)).start()
    copy(fine.at[hi], far_f.at[hi], y_send.at[3], y_recv.at[3, 1], ydev(-1)).start()

    def fine_done():
        arrived(far_f.at[lo], y_send.at[3], y_recv.at[3, 0], ydev(-1))
        arrived(far_f.at[hi], y_send.at[3], y_recv.at[3, 1], ydev(1))
        copy(far_f, far_f, y_send.at[3], y_recv.at[3, 0], ydev(1)).wait_send()

    rr = line(rr)
    sent_r = apply(1, xe1, ag1, plan, (), (y_up, y_down))

    def image(g, acc, ag):
        r = rows_of(g)
        nr, ni = total_of(g)
        vr, vi = R[0, r, :], R[1, r, :]
        wr, wi = 0.5 * vr + nr, 0.5 * vi + ni
        W[0, r, :] = wr
        W[1, r, :] = wi
        put_low(wr, wi, g, xe0, ag)
        return acc[0] + fold(vr * wr + vi * wi), acc[1] + fold(vr * wi - vi * wr)

    acc = lax.fori_loop(0, 4, lambda g, a: image(g, a, ag0), (zero8,) * 2)
    plan = gather(0, ag0, xe0)
    for s in plan[0]:
        s()
    pr, pi = lax.fori_loop(4, NB, lambda g, a: image(g, a, None), acc)
    halo_fronts(0, xe0)
    halo_start(0, xe0, 0)
    sum_cols, sum_end = clu_sum(0, [rr, line(pr), line(pi)])
    y_first, y_up, y_down, w_done = far_steps(2, xe0, far_w)
    y_first()

    sent_w = apply(0, xe0, ag0, plan, (), (sum_cols, y_up, y_down))
    rr, pr, pi = sum_end()
    beta2 = rr + EPS
    h11r, h11i = pr / beta2, pi / beta2

    def heights(g, acc):
        r = rows_of(g)
        nr, ni = total_of(g)
        vr, vi, wr, wi = R[0, r, :], R[1, r, :], W[0, r, :], W[1, r, :]
        ur = 0.5 * wr + nr - (h11r * wr - h11i * wi)
        ui = 0.5 * wi + ni - (h11r * wi + h11i * wr)
        wr, wi = wr - (h11r * vr - h11i * vi), wi - (h11r * vi + h11i * vr)
        W[0, r, :] = wr
        W[1, r, :] = wi
        new = (wr * wr + wi * wi, vr * wr + vi * wi, vr * wi - vi * wr,
               vr * ur + vi * ui, vr * ui - vi * ur, wr * ur + wi * ui, wr * ui - wi * ur, ur * ur + ui * ui)
        return tuple(a + fold(n) for a, n in zip(acc, new))

    sums = lax.fori_loop(0, NB, heights, (zero8,) * 8)
    allbuf[me] = jnp.concatenate([line(v) for v in sums], axis=0)
    for i in range(1, 32):
        peer = dev(lax.rem(me + i, 32))
        copy(allbuf.at[me], allbuf.at[me], col_send.at[1], col_recv.at[1], peer).start()
    rest31 = allbuf.at[pl.ds(0, 31)]
    copy(rest31, rest31, col_send.at[1], col_recv.at[1], dev(right)).wait()
    terms = [allbuf[i] for i in range(32)]
    while len(terms) > 1:
        terms = [a + b for a, b in zip(terms[::2], terms[1::2])]
    ww, gr, gi, ar, ai, br, bi, uu = [terms[0][i:i + 1, :] for i in range(8)]

    beta = jnp.sqrt(beta2)
    inv_b = 1.0 / beta
    h21 = jnp.sqrt(ww / beta2 + EPS)
    scale2 = inv_b / h21
    n1, n2 = rr * (inv_b * inv_b), ww * (scale2 * scale2)
    cross = inv_b * scale2
    h12r, h12i, g12r, g12i = ar * cross, ai * cross, gr * cross, gi * cross
    sq2 = scale2 * scale2
    h22r, h22i, un = br * sq2, bi * sq2, uu * sq2
    m12, m22 = h12r * h12r + h12i * h12i, h22r * h22r + h22i * h22i
    mixr, mixi = h12r * h22r + h12i * h22i, h12r * h22i - h12i * h22r
    rest = un + m12 * (n1 - 2.0) + m22 * (n2 - 2.0) + 2.0 * (mixr * g12r - mixi * g12i)
    h32 = jnp.sqrt(jnp.maximum(rest, 0.0) + EPS)

    r_one = jnp.sqrt(h11r * h11r + h11i * h11i + h21 * h21)
    q_real, q_imag, q_low = h11r / r_one, h11i / r_one, h21 / r_one
    mix_real = q_real * h12r + q_imag * h12i + q_low * h22r
    mix_imag = q_real * h12i - q_imag * h12r + q_low * h22i
    top_real = h12r - (mix_real * q_real - mix_imag * q_imag)
    top_imag = h12i - (mix_real * q_imag + mix_imag * q_real)
    mid_real, mid_imag = h22r - mix_real * q_low, h22i - mix_imag * q_low
    r_two_sq = top_real**2 + top_imag**2 + mid_real**2 + mid_imag**2 + h32 * h32
    y2r, y2i = beta * top_real / r_two_sq, -beta * top_imag / r_two_sq
    y1r = (beta * q_real - (mix_real * y2r - mix_imag * y2i)) / r_one
    y1i = (-beta * q_imag - (mix_real * y2i + mix_imag * y2r)) / r_one
    a1r, a1i, a2r, a2i = y1r * inv_b, y1i * inv_b, y2r * scale2, y2i * scale2

    ones = jnp.ones((1, BLK), F32)
    blank = jnp.zeros((1, BLK), F32)
    b1r, b1i = a1r - (a2r * h11r - a2i * h11i), a1i - (a2r * h11i + a2i * h11r)
    gbuf[yy] = jnp.concatenate([b1r, b1i, a2r, a2i, own_pr * ones, own_pi * ones, blank, blank], axis=0)
    for d in (1, 2, 3):
        copy(gbuf.at[yy], gbuf.at[yy], g_send.at[0], g_recv.at[0], ydev(d)).start()

    def solve(g, carry):
        r = rows_of(g)
        vr, vi, wr, wi = R[0, r, :], R[1, r, :], W[0, r, :], W[1, r, :]
        X0[0, r, :] = X0[0, r, :] + (a1r * vr - a1i * vi) + (a2r * wr - a2i * wi)
        X0[1, r, :] = X0[1, r, :] + (a1r * vi + a1i * vr) + (a2r * wi + a2i * wr)
        return carry

    lax.fori_loop(0, NB, solve, 0)
    out_scat = pltpu.make_async_copy(X0, scat_hbm, out_sem.at[0])
    out_scat.start()
    share_done()
    r_done()
    fine_done()
    w_done()
    sent_r()
    sent_w()
    three = gbuf.at[pl.ds(0, 3)]
    copy(three, three, g_send.at[0], g_recv.at[0], ydev(1)).wait()

    own_cr, own_ci = coef(yy, yy, own_pr, own_pi)
    factors = []
    for d in (-1, 1, 2):
        f = add4(yy, d)
        b = gbuf[f]
        cr, ci = coef(yy, f, b[4:5, :], b[5:6, :])
        for k in (0, 2):
            er, ei = b[k:k + 1, :], b[k + 1:k + 2, :]
            factors.append((cr * er + ci * ei, ci * er - cr * ei))

    def load_block(store, g):
        return store[pl.ds(2 * g, 2)].reshape(BLK, 2 * BLK).astype(F32)

    def trace(g, nearest):
        r = rows_of(g)
        t = full_in[0, r, :] + full_in[1, r, :] + (own_cr * X0[0, r, :] + own_ci * X0[1, r, :])
        for i in range(3):
            for k, store in enumerate((far_r, far_w)):
                v = load_block(store.at[i], g)
                if k == 0 and i == nearest:
                    v = v + load_block(far_f, g)
                fr, fi = factors[2 * i + k]
                t = t + (fr * v[:, :BLK] + fi * v[:, BLK:])
        part2[r, :] = t
        return 0

    lax.fori_loop(0, NB // 2, lambda g, _: trace(g, 0), 0)
    lax.fori_loop(NB // 2, NB, lambda g, _: trace(g, 1), 0)
    out_trace = pltpu.make_async_copy(part2, trace_hbm, out_sem.at[1])
    out_trace.start()
    out_scat.wait()
    out_trace.wait()


def local(incident, initial, near_blocks, near_pattern, crack_blocks, crack_cluster, crack_source, crack_target, pulse):
    vmem, dma = pltpu.VMEM, pltpu.SemaphoreType.DMA
    hbm, smem = pl.BlockSpec(memory_space=pl.ANY), pl.BlockSpec(memory_space=pltpu.SMEM)
    vec = (2, PANELS, BLK)
    scratch = [
        vmem((NB * NEAR, 2 * BLK, BLK), BF16),
        vmem((EDGES, 2 * BLK, BLK), BF16),
        vmem(vec, F32), vmem(vec, F32), vmem(vec, F32), vmem(vec, F32),
        vmem((EDGES + 1, BLK, 2 * BLK), F32),
        vmem((3 * SPAN, HALF, 2 * BLK), BF16), vmem((3 * SPAN, HALF, 2 * BLK), BF16),
        vmem((32 * SET, HALF, 2 * BLK), BF16), vmem((32 * SET, HALF, 2 * BLK), BF16),
        vmem((PANELS, BLK), F32), vmem((PANELS, BLK), F32), vmem((PANELS, BLK), F32),
        vmem((2, PANELS // 2, BLK), F32), vmem((2, PANELS, BLK), F32),
        vmem((3, SPAN, HALF, 2 * BLK), BF16), vmem((3, SPAN, HALF, 2 * BLK), BF16),
        vmem((SPAN, HALF, 2 * BLK), BF16), vmem((SPAN, HALF, 2 * BLK), BF16),
        vmem((1, 8, 8, BLK), F32), vmem((1, 4, 8, BLK), F32), vmem((4, 8, BLK), F32), vmem((32, 8, BLK), F32),
        dma((4,)), dma((2,)), dma((2, 44)), dma((2,)), dma((2,)), dma((2, 2)), dma((2,)),
        dma((4, 4)), dma((5,)), dma((2,)), dma((2,)), dma((2,)), dma((2,)), dma((1,)), dma((1,)),
    ]
    place = jnp.arange(EDGES + NB, dtype=I32)
    target = jnp.where(place < EDGES, jnp.pad(crack_target, (0, NB)), place - EDGES)
    each = jnp.arange(EDGES, dtype=I32)
    found = (crack_target[None, :] == target[:, None]) & (each[None, :] < place[:, None])
    links = jnp.max(jnp.where(found, each[None, :], -1), axis=1)
    links = jnp.where(links < 0, EDGES, links)
    scattered, trace = pl.pallas_call(
        kernel,
        out_shape=(jax.ShapeDtypeStruct(vec, F32), jax.ShapeDtypeStruct((PANELS, BLK), F32)),
        in_specs=[smem] * 5 + [hbm] * 4,
        out_specs=(hbm, hbm),
        scratch_shapes=scratch,
        compiler_params=pltpu.CompilerParams(
            collective_id=0, has_side_effects=True, vmem_limit_bytes=66_000_000),
        name="gmres",
    )(
        near_pattern.T, crack_cluster.T, crack_source, links, pulse,
        incident.reshape(vec), initial.reshape(vec),
        near_blocks.reshape(NB * NEAR, 2 * BLK, BLK), crack_blocks.reshape(EDGES, 2 * BLK, BLK),
    )
    return scattered[None], trace[None]


def solution(mesh):
    in_specs = (
        P("frq", None, "clu", None),
        P("frq", None, "clu", None),
        P("clu", None, "frq", None, None, None),
        P("clu", None),
        P("clu", "frq", None, None, None),
        P("clu", None),
        P("clu"),
        P("clu"),
        P("frq", None),
    )
    out_specs = (P("frq", None, "clu", None), P("frq", "clu", None))
    return jax.shard_map(local, mesh=mesh, in_specs=in_specs, out_specs=out_specs, check_vma=False)
```
